256 devices in a mesh: section: 8 (over y, core), dp: 32 (over z, x).
Axes of the slice: x: 4, y: 4, z: 8, core: 2. Of those that a mesh axis runs over, the one named last changes fastest.
Arguments:
- inputs: bfloat16 [5120, 2560], P('dp'), may hold values from -6 to 6
- cotangent: bfloat16 [5120, 2560], P('dp'), may hold values from -6 to 6
- weights: bfloat16 [8, 2560, 2560], P('section', 'dp'), may hold values from -0.0625 to 0.0625
- lengths: int32 [160], P('dp'), may hold values from 1 to 32, as said below
Outputs:
- pre_inputs: bfloat16 [8, 5120, 2560], P('section', 'dp')
- pre_grads: bfloat16 [8, 5120, 2560], P('section', 'dp')
The draws below stay inside these ranges and needn't reach their ends.
Inputs may be any that keep to these rules, and one draw needn't show every extreme that they name: `lengths`: each micro-batch has at least one live token; some micro-batch is full and some has exactly one.
All inputs are finite; a program needn't handle non-finite values.
Results may differ from the reference program's by a relative error of at most 0.012.
Values may be sent and summed in bfloat16 or wider, within the bound.
No kernel may reach another device: no remote copies, remote signals or barrier semaphores. Data moves between devices by JAX's collectives and lax.ppermute only.
A program may use at most 64 MiB of HBM per device.

```python
import jax
import jax.numpy as jnp
from jax import lax

D = 2560
BLOCK = 160
MB = 32
TOKENS = 5120
SECTIONS = 8


def draw_lengths(key, part):
    base = jax.random.randint(key, (TOKENS // MB,), 1, MB + 1)
    base = base.at[0].set(MB)
    return base.at[-1].set(1).astype(jnp.int32)


def block_levels(rng, extent, cuts, least, largest):
    factor_of = 1.0
    for dim, shards_of in cuts:
        heights = jax.random.uniform(jax.random.fold_in(jax.random.fold_in(rng, 6), dim), (shards_of,), jnp.float32, least / len(cuts), largest / len(cuts))
        factor_of = factor_of * jnp.repeat(jnp.exp(heights), extent[dim] // shards_of).reshape((-1,) + (1,) * (len(extent) - 1 - dim))
    return factor_of


def normal_values(key, dims, spread, bound, split=(), held_as=jnp.bfloat16):
    gain = block_levels(key, dims, split, -0.22, 0.18) if split else 1.0
    values = jax.random.normal(key, dims, jnp.float32) * spread * gain
    return jnp.minimum(jnp.maximum(values, -bound), bound).astype(held_as)


def setup_inputs(seed: int = 0) -> dict:
    seeds = jax.random.split(jax.random.key(seed), 5)
    return {
        "inputs": normal_values(seeds[0], (TOKENS, D), 1.0, 6.0, ((0, 32),)),
        "cotangent": normal_values(seeds[1], (TOKENS, D), 1.0, 6.0, ((0, 32),)),
        "weights": normal_values(seeds[2], (SECTIONS, D, D), (4 * D) ** -0.5, 0.0625, ((0, 8), (1, 32))),
        "lengths": draw_lengths(jax.random.fold_in(seeds[4], 71), 0),
    }


epsilon = 1e-05
damping = 0.1

def normalize(hidden):
    wide = hidden.astype(jnp.float32)
    factor = lax.rsqrt(lax.optimization_barrier(jnp.mean(wide * wide, axis=-1, keepdims=True)) + epsilon)
    return (wide * factor, factor)

def invert_blocks(blocks, counted):
    order = blocks.shape[-1]
    identity = jnp.eye(order, dtype=jnp.float32)
    damped = blocks / counted + damping * identity
    lower = jnp.linalg.cholesky(damped)
    half_way = lax.linalg.triangular_solve(lower, jnp.broadcast_to(identity, damped.shape), left_side=True, lower=True)
    inverse = lax.linalg.triangular_solve(lower, half_way, left_side=True, lower=True, transpose_a=True)
    return inverse.astype(jnp.bfloat16)

def gram_blocks(values, live):
    masked = jnp.where(live, values, jnp.zeros((), values.dtype)).astype(jnp.float32)
    shaped = masked.reshape(values.shape[0], D // BLOCK, BLOCK)
    return jnp.einsum('tbi,tbj->bij', shaped, shaped, precision=lax.Precision.HIGHEST)

def apply_blocks(values, inverse):
    shaped = values.astype(jnp.float32).reshape(values.shape[0], D // BLOCK, BLOCK)
    result = jnp.einsum('tbi,bij->tbj', shaped, inverse.astype(jnp.float32), precision=lax.Precision.HIGHEST)
    return result.reshape(values.shape[0], D).astype(jnp.bfloat16)

def reference(inputs, cotangent, weights, lengths):
    hidden = inputs
    hiddens = []
    activations = []
    for layer in range(SECTIONS):
        hiddens.append(hidden)
        normed, factor = normalize(hidden)
        activation = normed.astype(jnp.bfloat16)
        activations.append(activation)
        hidden = (hidden.astype(jnp.float32) + jnp.dot(activation.astype(jnp.float32), weights[layer].astype(jnp.float32), preferred_element_type=jnp.float32)).astype(jnp.bfloat16)
    gradients = [None] * SECTIONS
    current = cotangent
    for layer in range(SECTIONS - 1, -1, -1):
        gradients[layer] = current
        if layer > 0:
            normed, factor = normalize(hiddens[layer])
            back = jnp.dot(current.astype(jnp.float32), weights[layer].T.astype(jnp.float32), preferred_element_type=jnp.float32)
            through = factor * (back - normed * lax.optimization_barrier(jnp.mean(back * normed, axis=-1, keepdims=True)))
            current = (current.astype(jnp.float32) + through).astype(jnp.bfloat16)
    live = (jnp.arange(MB)[None, :] < lengths[:, None]).reshape(TOKENS, 1)
    counted = jnp.sum(live.astype(jnp.float32))
    first_out = []
    second_out = []
    for layer in range(SECTIONS):
        inverse_a = invert_blocks(gram_blocks(activations[layer], live), counted)
        inverse_g = invert_blocks(gram_blocks(gradients[layer], live), counted)
        first_out.append(apply_blocks(activations[layer], inverse_a))
        second_out.append(apply_blocks(gradients[layer], inverse_g))
    return (jnp.stack(first_out), jnp.stack(second_out))
```

```python
import jax
import jax.numpy as jnp
from jax import lax
from jax.experimental import pallas as pl
from jax.experimental.pallas import tpu as pltpu
from jax.sharding import PartitionSpec as P

BLOCK = 160
EPSILON = 1e-05
DAMPING = 0.1
LANES = 128
TILE = 256

f32 = jnp.float32
bf16 = jnp.bfloat16


def row_factor(own, other, width):
    total = jnp.sum(own * own, axis=-1, keepdims=True)
    total = total + jnp.sum(other * other, axis=-1, keepdims=True)
    return lax.rsqrt(total / width + EPSILON)


def forward_kernel(core_ref, own_ref, other_ref, wown_ref, wother_ref, out_ref, aown, aother):
    step = pl.program_id(0)
    half = own_ref.shape[1]

    @pl.when(step == 0)
    def _():
        own = own_ref[...].astype(f32)
        other = other_ref[...].astype(f32)
        factor = row_factor(own, other, 2 * half)
        aown[...] = (own * factor).astype(bf16)
        aother[...] = (other * factor).astype(bf16)

    result = jnp.dot(aown[...], wown_ref[...], preferred_element_type=f32)
    result = result + jnp.dot(aother[...], wother_ref[...], preferred_element_type=f32)
    columns = pl.ds(pl.multiple_of(step * TILE, TILE), TILE)
    out_ref[...] = (own_ref[:, columns].astype(f32) + result).astype(bf16)


def forward_layer(core, own, other, weight, which):
    rows, half = own.shape
    steps = half // TILE
    whole = pl.BlockSpec((rows, half), lambda i, c: (0, 0))
    return pl.pallas_call(
        forward_kernel,
        out_shape=jax.ShapeDtypeStruct((rows, half), bf16),
        grid_spec=pltpu.PrefetchScalarGridSpec(
            num_scalar_prefetch=1,
            grid=(steps,),
            in_specs=[
                whole,
                whole,
                pl.BlockSpec((half, TILE), lambda i, c: (c[0], which * steps + i)),
                pl.BlockSpec((half, TILE), lambda i, c: (1 - c[0], which * steps + i)),
            ],
            out_specs=pl.BlockSpec((rows, TILE), lambda i, c: (0, i)),
            scratch_shapes=[pltpu.VMEM((rows, half), bf16), pltpu.VMEM((rows, half), bf16)],
        ),
        cost_estimate=pl.CostEstimate(
            flops=4 * rows * half * half, bytes_accessed=4 * half * half, transcendentals=0
        ),
    )(core, own, other, weight, weight)


def backward_kernel(core_ref, grad_ref, own_ref, other_ref, weight_ref, send_ref, keep_ref, factor):
    step = pl.program_id(0)
    half = own_ref.shape[1]
    steps = half // TILE

    @pl.when(step == 0)
    def _():
        own = own_ref[...].astype(f32)
        other = other_ref[...].astype(f32)
        factor[...] = jnp.broadcast_to(row_factor(own, other, 2 * half), factor.shape)
        send_ref[:, half:] = jnp.zeros((own.shape[0], LANES), f32)

    part = lax.dot_general(
        grad_ref[...], weight_ref[...], (((1,), (1,)), ((), ())), preferred_element_type=f32
    )

    def along(hidden_ref, columns):
        product = part * hidden_ref[:, columns].astype(f32)
        send_ref[:, half:] += (product[:, :LANES] + product[:, LANES:]) * factor[...]

    @pl.when(step < steps)
    def _():
        columns = pl.ds(pl.multiple_of(step * TILE, TILE), TILE)
        along(other_ref, columns)
        send_ref[:, columns] = part

    @pl.when(step >= steps)
    def _():
        columns = pl.ds(pl.multiple_of((step - steps) * TILE, TILE), TILE)
        along(own_ref, columns)
        keep_ref[:, columns] = part


def backward_layer(core, grad, own, other, weight, which):
    rows, half = own.shape
    steps = half // TILE
    whole = pl.BlockSpec((rows, half), lambda i, c: (0, 0))

    def place(i, c):
        return (jnp.where(i < steps, (1 - c[0]) * steps + i, c[0] * steps + i - steps), which)

    send, keep = pl.pallas_call(
        backward_kernel,
        out_shape=[
            jax.ShapeDtypeStruct((rows, half + LANES), f32),
            jax.ShapeDtypeStruct((rows, half), f32),
        ],
        grid_spec=pltpu.PrefetchScalarGridSpec(
            num_scalar_prefetch=1,
            grid=(2 * steps,),
            in_specs=[whole, whole, whole, pl.BlockSpec((TILE, half), place)],
            out_specs=[pl.BlockSpec((rows, half + LANES), lambda i, c: (0, 0)), whole],
            scratch_shapes=[pltpu.VMEM((rows, LANES), f32)],
        ),
        cost_estimate=pl.CostEstimate(
            flops=4 * rows * half * half, bytes_accessed=4 * half * half, transcendentals=0
        ),
    )(core, grad, own, other, weight)
    arrived = swap_cores(send)
    width = 2 * half
    wide_own, wide_other = own.astype(f32), other.astype(f32)
    factor = row_factor(wide_own, wide_other, width)
    mean = jnp.sum(send[:, half:] + arrived[:, half:], axis=-1, keepdims=True) / width
    back = keep + arrived[:, :half]
    through = factor * (back - wide_own * factor * mean)
    return (grad.astype(f32) + through).astype(bf16)


PANEL = 32


def inverse_kernel(gram_ref, count_ref, out_ref, work):
    many, order = work.shape[0], work.shape[1]
    counted = count_ref[0]
    rows = lax.broadcasted_iota(jnp.int32, (order, order), 0)
    columns = lax.broadcasted_iota(jnp.int32, (order, order), 1)
    small_rows = lax.broadcasted_iota(jnp.int32, (PANEL, PANEL), 0)
    small_columns = lax.broadcasted_iota(jnp.int32, (PANEL, PANEL), 1)
    for m in range(many):
        total = gram_ref[0, m]
        for part in range(1, gram_ref.shape[0]):
            total = total + gram_ref[part, m]
        work[m] = total / counted + jnp.where(rows == columns, DAMPING, 0.0)
    for start in range(0, order, PANEL):
        stop = start + PANEL
        strips = [work[m, start:stop, :] for m in range(many)]
        pivots = [strip[:, start:stop] for strip in strips]
        for k in range(PANEL):
            keep = (small_rows != k) & (small_columns != k)
            for m in range(many):
                block = pivots[m]
                pivot = block[k : k + 1, k : k + 1]
                row = jnp.where(small_columns[:1] == k, -1.0, block[k : k + 1, :])
                column = jnp.where(small_rows[:, :1] == k, -1.0, block[:, k : k + 1])
                pivots[m] = jnp.where(keep, block, 0.0) - column * (row / pivot)
        inside_row = (rows >= start) & (rows < stop)
        inside_column = (columns >= start) & (columns < stop)
        strip_column = inside_column[:PANEL]
        unit = small_rows_eye(small_rows, columns[:PANEL], start)
        for m in range(many):
            strip = jnp.where(strip_column, unit, strips[m])
            solved = jnp.dot(
                -pivots[m], strip, precision=lax.Precision.HIGHEST, preferred_element_type=f32
            )
            change = lax.dot_general(
                strip,
                solved,
                (((0,), (0,)), ((), ())),
                precision=lax.Precision.HIGHEST,
                preferred_element_type=f32,
            )
            work[m] = jnp.where(inside_row | inside_column, 0.0, work[m]) - change
    for m in range(many):
        out_ref[m] = (-work[m]).astype(bf16)


def small_rows_eye(small_rows, wide_columns, start):
    rows = lax.broadcasted_iota(jnp.int32, wide_columns.shape, 0)
    return jnp.where(wide_columns == rows + start, -1.0, 0.0)


def invert_blocks(parts, counted):
    many, order = parts.shape[1], parts.shape[2]
    return pl.pallas_call(
        inverse_kernel,
        out_shape=jax.ShapeDtypeStruct((many, order, order), bf16),
        in_specs=[
            pl.BlockSpec(memory_space=pltpu.VMEM),
            pl.BlockSpec(memory_space=pltpu.SMEM),
        ],
        out_specs=pl.BlockSpec(memory_space=pltpu.VMEM),
        scratch_shapes=[pltpu.VMEM((many, order, order), f32)],
    )(parts, counted)


def swap_cores(array):
    count = lax.axis_size("section")
    return lax.ppermute(array, "section", [(i, i ^ 1) for i in range(count)])


def hop(array, source, by):
    pairs = [(2 * source + core, 2 * (source + by) + core) for core in range(2)]
    return lax.ppermute(array, "section", pairs)


def groups_along(count, stride, length):
    return [
        [base + stride * k for k in range(length)]
        for base in range(count)
        if (base // stride) % length == 0
    ]


def halves(core, own, other):
    first = jnp.where(core == 0, own, other)
    second = jnp.where(core == 0, other, own)
    return jnp.concatenate([first, second], axis=1)


def spread(values):
    lines = groups_along(lax.axis_size("dp"), 4, 8)
    return lax.all_to_all(
        values, "dp", split_axis=1, concat_axis=0, axis_index_groups=lines, tiled=True
    )


def gather_back(values):
    lines = groups_along(lax.axis_size("dp"), 4, 8)
    return lax.all_to_all(
        values, "dp", split_axis=0, concat_axis=1, axis_index_groups=lines, tiled=True
    )


def gram_parts(taken, live):
    blocks = taken.shape[1] // BLOCK
    masked = jnp.where(live, taken, jnp.zeros((), bf16))
    grams = []
    for b in range(blocks):
        part = masked[:, b * BLOCK : (b + 1) * BLOCK]
        grams.append(
            lax.dot_general(part, part, (((0,), (0,)), ((), ())), preferred_element_type=f32)
        )
    mates = groups_along(lax.axis_size("dp"), 1, 4)
    return lax.all_gather(jnp.stack(grams), "dp", axis=0, axis_index_groups=mates)


def apply_blocks(taken, inverse):
    blocks = inverse.shape[0]
    results = [
        jnp.dot(
            taken[:, b * BLOCK : (b + 1) * BLOCK], inverse[b], preferred_element_type=f32
        ).astype(bf16)
        for b in range(blocks)
    ]
    return jnp.concatenate(results, axis=1)


def on_device(inputs, cotangent, weights, lengths):
    section = lax.axis_index("section")
    chip, core = section // 2, section % 2
    chips = lax.axis_size("section") // 2
    tokens, width = inputs.shape
    half = width // 2
    batch_rows = tokens // lengths.shape[0]
    scalar_core = core.reshape(1).astype(jnp.int32)

    local = weights[0]
    mine = jnp.where(core == 0, local[:, :half], local[:, half:])
    theirs = jnp.where(core == 0, local[:, half:], local[:, :half])
    swapped = swap_cores(theirs)
    paired = halves(core, mine, swapped)
    weight = lax.all_gather(paired, "dp", axis=0, tiled=True)

    all_lengths = lax.all_gather(lengths, "dp", axis=0)
    alive = jnp.clip(all_lengths, 0, batch_rows)
    counted = jnp.sum(alive).astype(f32).reshape(1)
    across = lax.axis_index("dp") % 4
    line = lax.dynamic_index_in_dim(all_lengths.reshape(8, 4, -1), across, 1, keepdims=False)
    live = (jnp.arange(batch_rows)[None, :] < line.reshape(-1, 1)).reshape(-1, 1)

    def own_half(array):
        return jnp.where(core == 0, array[:, :half], array[:, half:])

    def other_half(array):
        return jnp.where(core == 0, array[:, half:], array[:, :half])

    first_own = own_half(inputs)
    empty = jnp.zeros((tokens, half), bf16)
    kept = (empty, empty, empty, empty)
    arriving = first_own
    for stage in range(chips):
        last = stage == chips - 1

        def turn(operands, stage=stage, last=last):
            own, weight = operands
            other = other_half(inputs) if stage == 0 else swap_cores(own)
            second = forward_layer(scalar_core, own, other, weight, 0)
            second_other = swap_cores(second)
            if last:
                leaving = empty
            else:
                leaving = forward_layer(scalar_core, second, second_other, weight, 1)
            return (own, other, second, second_other), leaving

        def rest(operands, kept=kept):
            return kept, empty

        kept, leaving = lax.cond(chip == stage, turn, rest, (arriving, weight))
        if not last:
            arriving = hop(leaving, stage, 1)

    own_a, other_a, own_b, other_b = kept
    grads = (empty, empty)
    arriving = own_half(cotangent)
    pre_inputs = None
    taken = None
    for stage in range(chips - 1, -1, -1):

        def turn(operands, stage=stage):
            grad, own_a, other_a, own_b, other_b, weight = operands
            grad_a = backward_layer(scalar_core, grad, own_b, other_b, weight, 1)
            if stage == 0:
                leaving = empty
            else:
                leaving = backward_layer(scalar_core, grad_a, own_a, other_a, weight, 0)
            return (grad_a, grad), leaving

        def rest(operands, grads=grads):
            return grads, empty

        grads, leaving = lax.cond(
            chip == stage, turn, rest, (arriving, own_a, other_a, own_b, other_b, weight)
        )
        if stage > 0:
            arriving = hop(leaving, stage, -1)
        if stage == chips - 1:
            own = jnp.where(core == 0, own_a, own_b)
            other = jnp.where(core == 0, other_a, other_b)
            own, other, leaving = lax.optimization_barrier((own, other, leaving))
            full = halves(core, own, other).astype(f32)
            mean = jnp.mean(full * full, axis=-1, keepdims=True)
            taken = spread((full * lax.rsqrt(mean + EPSILON)).astype(bf16))
            parts = gram_parts(taken, live)
            arriving, parts = lax.optimization_barrier((arriving, parts))
        elif stage == chips - 2:
            grads, parts = lax.optimization_barrier((grads, parts))
            inverse = invert_blocks(parts, counted)
            pre_inputs = gather_back(apply_blocks(taken, inverse))
            arriving, pre_inputs = lax.optimization_barrier((arriving, pre_inputs))

    grad_a, grad_b = grads
    own = jnp.where(core == 0, grad_a, grad_b)
    other = swap_cores(jnp.where(core == 0, grad_b, grad_a))
    taken = spread(halves(core, own, other))
    inverse = invert_blocks(gram_parts(taken, live), counted)
    pre_grads = gather_back(apply_blocks(taken, inverse))
    return (pre_inputs[None], pre_grads[None])


def solution(mesh):
    in_specs = (P("dp", None), P("dp", None), P("section", "dp", None), P("dp"))
    out_specs = (P("section", "dp", None), P("section", "dp", None))
    return jax.shard_map(
        on_device, mesh=mesh, in_specs=in_specs, out_specs=out_specs, check_vma=False
    )
```

```python
import functools

import jax
import jax.numpy as jnp
from jax import lax
from jax.experimental import pallas as pl
from jax.experimental.pallas import tpu as pltpu
from jax.sharding import PartitionSpec as P


BLOCK = 160
EPSILON = 1e-05
DAMPING = 0.1
LANES = 128
TILE = 640
ROWS = 640

f32 = jnp.float32
bf16 = jnp.bfloat16


def row_factor(own, other, width):
    total = jnp.sum(own * own, axis=-1, keepdims=True)
    total = total + jnp.sum(other * other, axis=-1, keepdims=True)
    return lax.rsqrt(total / width + EPSILON)


def forward_kernel(core_ref, own_ref, other_ref, wown_ref, wother_ref, out_ref, aown, aother):
    step = pl.program_id(0)
    half = own_ref.shape[1]

    @pl.when(step == 0)
    def _():
        own = own_ref[...].astype(f32)
        other = other_ref[...].astype(f32)
        factor = row_factor(own, other, 2 * half)
        aown[...] = (own * factor).astype(bf16)
        aother[...] = (other * factor).astype(bf16)

    result = jnp.dot(aown[...], wown_ref[...], preferred_element_type=f32)
    result = result + jnp.dot(aother[...], wother_ref[...], preferred_element_type=f32)
    columns = pl.ds(pl.multiple_of(step * TILE, TILE), TILE)
    out_ref[...] = (own_ref[:, columns].astype(f32) + result).astype(bf16)


def forward_layer(core, own, other, weight, which):
    rows, half = own.shape
    steps = half // TILE
    whole = pl.BlockSpec((rows, half), lambda i, c: (0, 0))
    return pl.pallas_call(
        forward_kernel,
        out_shape=jax.ShapeDtypeStruct((rows, half), bf16),
        grid_spec=pltpu.PrefetchScalarGridSpec(
            num_scalar_prefetch=1,
            grid=(steps,),
            in_specs=[
                whole,
                whole,
                pl.BlockSpec((half, TILE), lambda i, c: (c[0], which * steps + i)),
                pl.BlockSpec((half, TILE), lambda i, c: (1 - c[0], which * steps + i)),
            ],
            out_specs=pl.BlockSpec((rows, TILE), lambda i, c: (0, i)),
            scratch_shapes=[pltpu.VMEM((rows, half), bf16), pltpu.VMEM((rows, half), bf16)],
        ),
        cost_estimate=pl.CostEstimate(
            flops=4 * rows * half * half, bytes_accessed=4 * half * half, transcendentals=0
        ),
    )(core, own, other, weight, weight)


def finish(grad, keep, sent, arrived, own):
    half = own.shape[1]
    mean = jnp.sum(sent + arrived[:, half:], axis=-1, keepdims=True) / (2 * half)
    factor = keep[:, half : half + 1]
    back = keep[:, :half] + arrived[:, :half]
    through = factor * (back - own.astype(f32) * factor * mean)
    return (grad.astype(f32) + through).astype(bf16)


def finish_kernel(grad_ref, keep_ref, sent_ref, arrived_ref, own_ref, out_ref):
    out_ref[...] = finish(
        grad_ref[...], keep_ref[...], sent_ref[...], arrived_ref[...], own_ref[...]
    )


def finish_layer(grad, keep, send, arrived, own):
    rows, half = own.shape
    whole = pl.BlockSpec((rows, half), lambda i: (0, 0))
    wide = pl.BlockSpec((rows, half + LANES), lambda i: (0, 0))
    return pl.pallas_call(
        finish_kernel,
        out_shape=jax.ShapeDtypeStruct((rows, half), bf16),
        grid=(1,),
        in_specs=[whole, wide, pl.BlockSpec((rows, LANES), lambda i: (0, half // LANES)), wide, whole],
        out_specs=whole,
        cost_estimate=pl.CostEstimate(
            flops=8 * rows * half, bytes_accessed=16 * rows * half, transcendentals=0
        ),
    )(grad, keep, send, arrived, own)


def backward_kernel(fused, core_ref, *refs):
    if fused:
        before, refs = refs[:5], refs[5:]
        own_ref, other_ref, weight_ref, send_ref, keep_ref, grad_ref = refs
    else:
        grad_ref, own_ref, other_ref, weight_ref, send_ref, keep_ref = refs
    step = pl.program_id(0)
    rows, half = own_ref.shape
    steps = half // ROWS

    @pl.when(step == 0)
    def _():
        if fused:
            grad_ref[...] = finish(*[ref[...] for ref in before])
        own = own_ref[...].astype(f32)
        other = other_ref[...].astype(f32)
        keep_ref[:, half:] = jnp.broadcast_to(row_factor(own, other, 2 * half), (rows, LANES))
        send_ref[:, half:] = jnp.zeros((rows, LANES), f32)

    part = lax.dot_general(
        grad_ref[...], weight_ref[...], (((1,), (1,)), ((), ())), preferred_element_type=f32
    )

    def along(hidden_ref, columns):
        product = part * hidden_ref[:, columns].astype(f32)
        folded = product[:, :LANES]
        for k in range(1, ROWS // LANES):
            folded = folded + product[:, k * LANES : (k + 1) * LANES]
        send_ref[:, half:] += folded * keep_ref[:, half:]

    @pl.when(step < steps)
    def _():
        columns = pl.ds(pl.multiple_of(step * ROWS, LANES), ROWS)
        send_ref[:, columns] = part
        along(other_ref, columns)

    @pl.when(step >= steps)
    def _():
        columns = pl.ds(pl.multiple_of((step - steps) * ROWS, LANES), ROWS)
        keep_ref[:, columns] = part
        along(own_ref, columns)


def backward_layer(core, before, own, other, weight, which):
    rows, half = own.shape
    steps = half // ROWS
    fused = len(before) > 1
    whole = pl.BlockSpec((rows, half), lambda i, c: (0, 0))
    wide = pl.BlockSpec((rows, half + LANES), lambda i, c: (0, 0))
    tail = pl.BlockSpec((rows, LANES), lambda i, c: (0, half // LANES))

    def place(i, c):
        return (jnp.where(i < steps, (1 - c[0]) * steps + i, c[0] * steps + i - steps), which)

    out_shape = [jax.ShapeDtypeStruct((rows, half + LANES), f32)] * 2
    first = [whole, wide, tail, wide, whole] if fused else [whole]
    results = pl.pallas_call(
        functools.partial(backward_kernel, fused),
        out_shape=out_shape + [jax.ShapeDtypeStruct((rows, half), bf16)] * fused,
        grid_spec=pltpu.PrefetchScalarGridSpec(
            num_scalar_prefetch=1,
            grid=(2 * steps,),
            in_specs=first + [whole, whole, pl.BlockSpec((ROWS, half), place)],
            out_specs=[wide, wide] + [whole] * fused,
        ),
        cost_estimate=pl.CostEstimate(
            flops=4 * rows * half * half, bytes_accessed=4 * half * half, transcendentals=0
        ),
    )(core, *before, own, other, weight)
    send, keep = results[:2]
    grad = results[2] if fused else before[0]
    return (grad, keep, send, swap_cores(send), own)


PANEL = 32


def inverse_kernel(gram_ref, count_ref, out_ref, work):
    many, order = work.shape[0], work.shape[1]
    counted = count_ref[0]
    rows = lax.broadcasted_iota(jnp.int32, (order, order), 0)
    columns = lax.broadcasted_iota(jnp.int32, (order, order), 1)
    small_rows = lax.broadcasted_iota(jnp.int32, (PANEL, PANEL), 0)
    small_columns = lax.broadcasted_iota(jnp.int32, (PANEL, PANEL), 1)
    for m in range(many):
        total = gram_ref[0, m]
        for part in range(1, gram_ref.shape[0]):
            total = total + gram_ref[part, m]
        work[m] = total / counted + jnp.where(rows == columns, DAMPING, 0.0)
    for start in range(0, order, PANEL):
        stop = start + PANEL
        strips = [work[m, start:stop, :] for m in range(many)]
        pivots = [strip[:, start:stop] for strip in strips]
        for k in range(PANEL):
            keep = (small_rows != k) & (small_columns != k)
            for m in range(many):
                block = pivots[m]
                pivot = block[k : k + 1, k : k + 1]
                row = jnp.where(small_columns[:1] == k, -1.0, block[k : k + 1, :])
                column = jnp.where(small_rows[:, :1] == k, -1.0, block[:, k : k + 1])
                pivots[m] = jnp.where(keep, block, 0.0) - column * (row / pivot)
        inside_row = (rows >= start) & (rows < stop)
        inside_column = (columns >= start) & (columns < stop)
        strip_column = inside_column[:PANEL]
        unit = small_rows_eye(columns[:PANEL], start)
        for m in range(many):
            strip = jnp.where(strip_column, unit, strips[m])
            solved = jnp.dot(
                -pivots[m], strip, precision=lax.Precision.HIGHEST, preferred_element_type=f32
            )
            change = lax.dot_general(
                strip,
                solved,
                (((0,), (0,)), ((), ())),
                precision=lax.Precision.HIGHEST,
                preferred_element_type=f32,
            )
            work[m] = jnp.where(inside_row | inside_column, 0.0, work[m]) - change
    for m in range(many):
        out_ref[m] = (-work[m]).astype(bf16)


def small_rows_eye(wide_columns, start):
    rows = lax.broadcasted_iota(jnp.int32, wide_columns.shape, 0)
    return jnp.where(wide_columns == rows + start, -1.0, 0.0)


def invert_blocks(parts, counted):
    many, order = parts.shape[1], parts.shape[2]
    return pl.pallas_call(
        inverse_kernel,
        out_shape=jax.ShapeDtypeStruct((many, order, order), bf16),
        in_specs=[
            pl.BlockSpec(memory_space=pltpu.VMEM),
            pl.BlockSpec(memory_space=pltpu.SMEM),
        ],
        out_specs=pl.BlockSpec(memory_space=pltpu.VMEM),
        scratch_shapes=[pltpu.VMEM((many, order, order), f32)],
    )(parts, counted)


def swap_cores(array):
    count = lax.axis_size("section")
    return lax.ppermute(array, "section", [(i, i ^ 1) for i in range(count)])


def hop(array, source, by):
    pairs = [(2 * source + core, 2 * (source + by) + core) for core in range(2)]
    return lax.ppermute(array, "section", pairs)


def groups_along(count, stride, length):
    return [
        [base + stride * k for k in range(length)]
        for base in range(count)
        if (base // stride) % length == 0
    ]


def halves(core, own, other):
    first = jnp.where(core == 0, own, other)
    second = jnp.where(core == 0, other, own)
    return jnp.concatenate([first, second], axis=1)


def spread(values):
    lines = groups_along(lax.axis_size("dp"), 4, 8)
    return lax.all_to_all(
        values, "dp", split_axis=1, concat_axis=0, axis_index_groups=lines, tiled=True
    )


def gather_back(values):
    lines = groups_along(lax.axis_size("dp"), 4, 8)
    return lax.all_to_all(
        values, "dp", split_axis=0, concat_axis=1, axis_index_groups=lines, tiled=True
    )


def gram_parts(taken, live):
    blocks = taken.shape[1] // BLOCK
    masked = jnp.where(live, taken, jnp.zeros((), bf16))
    grams = []
    for b in range(blocks):
        part = masked[:, b * BLOCK : (b + 1) * BLOCK]
        grams.append(
            lax.dot_general(part, part, (((0,), (0,)), ((), ())), preferred_element_type=f32)
        )
    mates = groups_along(lax.axis_size("dp"), 1, 4)
    return lax.all_gather(jnp.stack(grams), "dp", axis=0, axis_index_groups=mates)


def apply_blocks(taken, inverse):
    blocks = inverse.shape[0]
    results = [
        jnp.dot(
            taken[:, b * BLOCK : (b + 1) * BLOCK], inverse[b], preferred_element_type=f32
        ).astype(bf16)
        for b in range(blocks)
    ]
    return jnp.concatenate(results, axis=1)


def all_stages(inputs, cotangent, weights, lengths):
    section = lax.axis_index("section")
    chip, core = section // 2, section % 2
    chips = lax.axis_size("section") // 2
    tokens, width = inputs.shape
    half = width // 2
    batch_rows = tokens // lengths.shape[0]
    scalar_core = core.reshape(1).astype(jnp.int32)

    local = weights[0]
    mine = jnp.where(core == 0, local[:, :half], local[:, half:])
    theirs = jnp.where(core == 0, local[:, half:], local[:, :half])
    swapped = swap_cores(theirs)
    paired = halves(core, mine, swapped)
    weight = lax.all_gather(paired, "dp", axis=0, tiled=True)

    all_lengths = lax.all_gather(lengths, "dp", axis=0)
    alive = jnp.clip(all_lengths, 0, batch_rows)
    counted = jnp.sum(alive).astype(f32).reshape(1)
    across = lax.axis_index("dp") % 4
    line = lax.dynamic_index_in_dim(all_lengths.reshape(8, 4, -1), across, 1, keepdims=False)
    live = (jnp.arange(batch_rows)[None, :] < line.reshape(-1, 1)).reshape(-1, 1)

    def own_half(array):
        return jnp.where(core == 0, array[:, :half], array[:, half:])

    def other_half(array):
        return jnp.where(core == 0, array[:, half:], array[:, :half])

    first_own = own_half(inputs)
    first_own, counted, live = lax.optimization_barrier((first_own, counted, live))
    empty = jnp.zeros((tokens, half), bf16)
    kept = (empty, empty, empty, empty)
    arriving = first_own
    for stage in range(chips):
        last = stage == chips - 1

        def turn(operands, stage=stage, last=last):
            own, weight = operands
            other = other_half(inputs) if stage == 0 else swap_cores(own)
            second = forward_layer(scalar_core, own, other, weight, 0)
            second_other = swap_cores(second)
            if last:
                leaving = empty
            else:
                leaving = forward_layer(scalar_core, second, second_other, weight, 1)
            return (own, other, second, second_other), leaving

        def rest(operands, kept=kept):
            return kept, empty

        kept, leaving = lax.cond(chip == stage, turn, rest, (arriving, weight))
        if not last:
            arriving = hop(leaving, stage, 1)

    own_a, other_a, own_b, other_b = kept
    grads = (empty, empty)
    arriving = own_half(cotangent)
    pre_inputs = None
    taken = None
    for stage in range(chips - 1, -1, -1):

        def turn(operands, stage=stage):
            grad, own_a, other_a, own_b, other_b, weight = operands
            pieces = backward_layer(scalar_core, (grad,), own_b, other_b, weight, 1)
            if stage == 0:
                return (finish_layer(*pieces), grad), empty
            pieces = backward_layer(scalar_core, pieces, own_a, other_a, weight, 0)
            return (pieces[0], grad), finish_layer(*pieces)

        def rest(operands, grads=grads):
            return grads, empty

        grads, leaving = lax.cond(
            chip == stage, turn, rest, (arriving, own_a, other_a, own_b, other_b, weight)
        )
        if stage > 0:
            arriving = hop(leaving, stage, -1)
        if stage == chips - 1:
            own = jnp.where(core == 0, own_a, own_b)
            other = jnp.where(core == 0, other_a, other_b)
            own, other, leaving = lax.optimization_barrier((own, other, leaving))
            full = halves(core, own, other).astype(f32)
            mean = jnp.mean(full * full, axis=-1, keepdims=True)
            full = (full * lax.rsqrt(mean + EPSILON)).astype(bf16)
            taken = spread(full)
            parts = gram_parts(taken, live)
            arriving, parts = lax.optimization_barrier((arriving, parts))
        elif stage == chips - 2:
            grads, parts = lax.optimization_barrier((grads, parts))
            inverse = invert_blocks(parts, counted)
            pre_inputs = gather_back(apply_blocks(taken, inverse))
            arriving, pre_inputs = lax.optimization_barrier((arriving, pre_inputs))

    grad_a, grad_b = grads
    own = jnp.where(core == 0, grad_a, grad_b)
    other = swap_cores(jnp.where(core == 0, grad_b, grad_a))
    taken = spread(halves(core, own, other))
    inverse = invert_blocks(gram_parts(taken, live), counted)
    pre_grads = gather_back(apply_blocks(taken, inverse))
    return (pre_inputs[None], pre_grads[None])


def solution(mesh):
    in_specs = (P("dp", None), P("dp", None), P("section", "dp", None), P("dp"))
    out_specs = (P("section", "dp", None), P("section", "dp", None))
    return jax.shard_map(
        all_stages, mesh=mesh, in_specs=in_specs, out_specs=out_specs, check_vma=False
    )
```

```python
import functools

import jax
import jax.numpy as jnp
from jax import lax
from jax.experimental import pallas as pl
from jax.experimental.pallas import tpu as pltpu
from jax.sharding import PartitionSpec as P


BLOCK = 160
EPSILON = 1e-05
DAMPING = 0.1
LANES = 128
TILE = 640
ROWS = 640

f32 = jnp.float32
bf16 = jnp.bfloat16


def row_factor(own, other, width):
    total = jnp.sum(own * own, axis=-1, keepdims=True)
    total = total + jnp.sum(other * other, axis=-1, keepdims=True)
    return lax.rsqrt(total / width + EPSILON)


def forward_kernel(core_ref, own_ref, other_ref, wown_ref, wother_ref, out_ref, aown, aother):
    step = pl.program_id(0)
    half = own_ref.shape[1]

    @pl.when(step == 0)
    def _():
        own = own_ref[...].astype(f32)
        other = other_ref[...].astype(f32)
        factor = row_factor(own, other, 2 * half)
        aown[...] = (own * factor).astype(bf16)
        aother[...] = (other * factor).astype(bf16)

    result = jnp.dot(aown[...], wown_ref[...], preferred_element_type=f32)
    result = result + jnp.dot(aother[...], wother_ref[...], preferred_element_type=f32)
    columns = pl.ds(pl.multiple_of(step * TILE, TILE), TILE)
    out_ref[...] = (own_ref[:, columns].astype(f32) + result).astype(bf16)


def forward_layer(core, own, other, weight, which):
    rows, half = own.shape
    steps = half // TILE
    whole = pl.BlockSpec((rows, half), lambda i, c: (0, 0))
    return pl.pallas_call(
        forward_kernel,
        out_shape=jax.ShapeDtypeStruct((rows, half), bf16),
        grid_spec=pltpu.PrefetchScalarGridSpec(
            num_scalar_prefetch=1,
            grid=(steps,),
            in_specs=[
                whole,
                whole,
                pl.BlockSpec((half, TILE), lambda i, c: (c[0], which * steps + i)),
                pl.BlockSpec((half, TILE), lambda i, c: (1 - c[0], which * steps + i)),
            ],
            out_specs=pl.BlockSpec((rows, TILE), lambda i, c: (0, i)),
            scratch_shapes=[pltpu.VMEM((rows, half), bf16), pltpu.VMEM((rows, half), bf16)],
        ),
        cost_estimate=pl.CostEstimate(
            flops=4 * rows * half * half, bytes_accessed=4 * half * half, transcendentals=0
        ),
    )(core, own, other, weight, weight)


def finish(grad, keep, sent, arrived, own):
    half = own.shape[1]
    mean = jnp.sum(sent + arrived[:, half:], axis=-1, keepdims=True) / (2 * half)
    factor = keep[:, half : half + 1]
    back = keep[:, :half] + arrived[:, :half]
    through = factor * (back - own.astype(f32) * factor * mean)
    return (grad.astype(f32) + through).astype(bf16)


def finish_kernel(grad_ref, keep_ref, sent_ref, arrived_ref, own_ref, out_ref):
    out_ref[...] = finish(
        grad_ref[...], keep_ref[...], sent_ref[...], arrived_ref[...], own_ref[...]
    )


def finish_layer(grad, keep, send, arrived, own):
    rows, half = own.shape
    whole = pl.BlockSpec((rows, half), lambda i: (0, 0))
    wide = pl.BlockSpec((rows, half + LANES), lambda i: (0, 0))
    return pl.pallas_call(
        finish_kernel,
        out_shape=jax.ShapeDtypeStruct((rows, half), bf16),
        grid=(1,),
        in_specs=[whole, wide, pl.BlockSpec((rows, LANES), lambda i: (0, half // LANES)), wide, whole],
        out_specs=whole,
        cost_estimate=pl.CostEstimate(
            flops=8 * rows * half, bytes_accessed=16 * rows * half, transcendentals=0
        ),
    )(grad, keep, send, arrived, own)


def backward_kernel(fused, core_ref, *refs):
    if fused:
        before, refs = refs[:5], refs[5:]
        own_ref, other_ref, weight_ref, send_ref, keep_ref, grad_ref = refs
    else:
        grad_ref, own_ref, other_ref, weight_ref, send_ref, keep_ref = refs
    step = pl.program_id(0)
    rows, half = own_ref.shape
    steps = half // ROWS

    @pl.when(step == 0)
    def _():
        if fused:
            grad_ref[...] = finish(*[ref[...] for ref in before])
        own = own_ref[...].astype(f32)
        other = other_ref[...].astype(f32)
        keep_ref[:, half:] = jnp.broadcast_to(row_factor(own, other, 2 * half), (rows, LANES))
        send_ref[:, half:] = jnp.zeros((rows, LANES), f32)

    part = lax.dot_general(
        grad_ref[...], weight_ref[...], (((1,), (1,)), ((), ())), preferred_element_type=f32
    )

    def along(hidden_ref, columns):
        product = part * hidden_ref[:, columns].astype(f32)
        folded = product[:, :LANES]
        for k in range(1, ROWS // LANES):
            folded = folded + product[:, k * LANES : (k + 1) * LANES]
        send_ref[:, half:] += folded * keep_ref[:, half:]

    @pl.when(step < steps)
    def _():
        columns = pl.ds(pl.multiple_of(step * ROWS, LANES), ROWS)
        send_ref[:, columns] = part
        along(other_ref, columns)

    @pl.when(step >= steps)
    def _():
        columns = pl.ds(pl.multiple_of((step - steps) * ROWS, LANES), ROWS)
        keep_ref[:, columns] = part
        along(own_ref, columns)


def backward_layer(core, before, own, other, weight, which):
    rows, half = own.shape
    steps = half // ROWS
    fused = len(before) > 1
    whole = pl.BlockSpec((rows, half), lambda i, c: (0, 0))
    wide = pl.BlockSpec((rows, half + LANES), lambda i, c: (0, 0))
    tail = pl.BlockSpec((rows, LANES), lambda i, c: (0, half // LANES))

    def place(i, c):
        return (jnp.where(i < steps, (1 - c[0]) * steps + i, c[0] * steps + i - steps), which)

    out_shape = [jax.ShapeDtypeStruct((rows, half + LANES), f32)] * 2
    first = [whole, wide, tail, wide, whole] if fused else [whole]
    results = pl.pallas_call(
        functools.partial(backward_kernel, fused),
        out_shape=out_shape + [jax.ShapeDtypeStruct((rows, half), bf16)] * fused,
        grid_spec=pltpu.PrefetchScalarGridSpec(
            num_scalar_prefetch=1,
            grid=(2 * steps,),
            in_specs=first + [whole, whole, pl.BlockSpec((ROWS, half), place)],
            out_specs=[wide, wide] + [whole] * fused,
        ),
        cost_estimate=pl.CostEstimate(
            flops=4 * rows * half * half, bytes_accessed=4 * half * half, transcendentals=0
        ),
    )(core, *before, own, other, weight)
    send, keep = results[:2]
    grad = results[2] if fused else before[0]
    return (grad, keep, send, swap_cores(send), own)


def inverse_kernel(first_ref, second_ref, count_ref, out_ref):
    order = out_ref.shape[0]
    rows = lax.broadcasted_iota(jnp.int32, (order, order), 0)
    columns = lax.broadcasted_iota(jnp.int32, (order, order), 1)
    row, column = columns[:1], rows[:, :1]
    block = (first_ref[...] + second_ref[...]) / count_ref[0]
    block = block + jnp.where(rows == columns, DAMPING, 0.0)
    for k in range(0, order, 2):
        n = k + 1
        a, b, c = block[k : k + 1, k : k + 1], block[k : k + 1, n : n + 1], block[n : n + 1, n : n + 1]
        scale = 1.0 / (a * c - b * b)
        row_k = jnp.where(row == k, -1.0, jnp.where(row == n, 0.0, block[k : k + 1, :]))
        row_n = jnp.where(row == n, -1.0, jnp.where(row == k, 0.0, block[n : n + 1, :]))
        column_k = jnp.where(column == k, -1.0, jnp.where(column == n, 0.0, block[:, k : k + 1]))
        column_n = jnp.where(column == n, -1.0, jnp.where(column == k, 0.0, block[:, n : n + 1]))
        solved_k = (c * row_k - b * row_n) * scale
        solved_n = (a * row_n - b * row_k) * scale
        outside = (rows // 2 != k // 2) & (columns // 2 != k // 2)
        block = jnp.where(outside, block, 0.0) - column_k * solved_k - column_n * solved_n
    out_ref[...] = (-block).astype(bf16)


def invert_block(first, second, counted):
    order = first.shape[0]
    return pl.pallas_call(
        inverse_kernel,
        out_shape=jax.ShapeDtypeStruct((order, order), bf16),
        in_specs=[
            pl.BlockSpec(memory_space=pltpu.VMEM),
            pl.BlockSpec(memory_space=pltpu.VMEM),
            pl.BlockSpec(memory_space=pltpu.SMEM),
        ],
        out_specs=pl.BlockSpec(memory_space=pltpu.VMEM),
    )(first, second, counted)


def swap_cores(array):
    count = lax.axis_size("section")
    return lax.ppermute(array, "section", [(i, i ^ 1) for i in range(count)])


def hop(array, source, by):
    pairs = [(2 * source + core, 2 * (source + by) + core) for core in range(2)]
    return lax.ppermute(array, "section", pairs)


GROUP = 8


def groups_near(count):
    return [list(range(base, base + GROUP)) for base in range(0, count, GROUP)]


def swap_groups(array, apart):
    count = lax.axis_size("dp")
    pairs = [(i, (i // GROUP ^ apart) * GROUP + i % GROUP) for i in range(count)]
    return lax.ppermute(array, "dp", pairs)


def halves(core, own, other):
    first = jnp.where(core == 0, own, other)
    second = jnp.where(core == 0, other, own)
    return jnp.concatenate([first, second], axis=1)


def spread(values):
    lines = groups_near(lax.axis_size("dp"))
    return lax.all_to_all(
        values, "dp", split_axis=1, concat_axis=0, axis_index_groups=lines, tiled=True
    )


def gather_back(values):
    lines = groups_near(lax.axis_size("dp"))
    return lax.all_to_all(
        values, "dp", split_axis=0, concat_axis=1, axis_index_groups=lines, tiled=True
    )


def gram_halves(taken, live, odd):
    masked = jnp.where(live, taken, jnp.zeros((), bf16))
    grams = []
    for b in range(2):
        part = masked[:, b * BLOCK : (b + 1) * BLOCK]
        grams.append(
            lax.dot_general(part, part, (((0,), (0,)), ((), ())), preferred_element_type=f32)
        )
    mine = jnp.where(odd, grams[1], grams[0])
    theirs = jnp.where(odd, grams[0], grams[1])
    return mine, theirs


def sum_and_invert(mine, theirs, counted, odd):
    paired = mine + swap_groups(theirs, 1)
    inverse = invert_block(paired, swap_groups(paired, 2), counted)
    other = swap_groups(inverse, 1)
    return jnp.where(odd, other, inverse), jnp.where(odd, inverse, other)


def apply_blocks(taken, inverses):
    results = [
        jnp.dot(
            taken[:, b * BLOCK : (b + 1) * BLOCK], inverse, preferred_element_type=f32
        ).astype(bf16)
        for b, inverse in enumerate(inverses)
    ]
    return jnp.concatenate(results, axis=1)


def all_stages(inputs, cotangent, weights, lengths):
    section = lax.axis_index("section")
    chip, core = section // 2, section % 2
    chips = lax.axis_size("section") // 2
    tokens, width = inputs.shape
    half = width // 2
    batch_rows = tokens // lengths.shape[0]
    scalar_core = core.reshape(1).astype(jnp.int32)

    local = weights[0]
    mine = jnp.where(core == 0, local[:, :half], local[:, half:])
    theirs = jnp.where(core == 0, local[:, half:], local[:, :half])
    swapped = swap_cores(theirs)
    paired = halves(core, mine, swapped)
    weight = lax.all_gather(paired, "dp", axis=0, tiled=True)

    all_lengths = lax.all_gather(lengths, "dp", axis=0)
    alive = jnp.clip(all_lengths, 0, batch_rows)
    counted = jnp.sum(alive).astype(f32).reshape(1)
    near = lax.axis_index("dp") // GROUP
    odd = near % 2 == 1
    line = lax.dynamic_index_in_dim(all_lengths.reshape(4, GROUP, -1), near, 0, keepdims=False)
    live = (jnp.arange(batch_rows)[None, :] < line.reshape(-1, 1)).reshape(-1, 1)

    def own_half(array):
        return jnp.where(core == 0, array[:, :half], array[:, half:])

    def other_half(array):
        return jnp.where(core == 0, array[:, half:], array[:, :half])

    first_own = own_half(inputs)
    first_own, counted, live = lax.optimization_barrier((first_own, counted, live))
    empty = jnp.zeros((tokens, half), bf16)
    kept = (empty, empty, empty, empty)
    arriving = first_own
    for stage in range(chips):
        last = stage == chips - 1

        def turn(operands, stage=stage, last=last):
            own, weight = operands
            other = other_half(inputs) if stage == 0 else swap_cores(own)
            second = forward_layer(scalar_core, own, other, weight, 0)
            second_other = swap_cores(second)
            if last:
                leaving = empty
            else:
                leaving = forward_layer(scalar_core, second, second_other, weight, 1)
            return (own, other, second, second_other), leaving

        def rest(operands, kept=kept):
            return kept, empty

        kept, leaving = lax.cond(chip == stage, turn, rest, (arriving, weight))
        if not last:
            arriving = hop(leaving, stage, 1)

    own_a, other_a, own_b, other_b = kept
    grads = (empty, empty)
    arriving = own_half(cotangent)
    pre_inputs = None
    taken = None
    for stage in range(chips - 1, -1, -1):

        def turn(operands, stage=stage):
            grad, own_a, other_a, own_b, other_b, weight = operands
            pieces = backward_layer(scalar_core, (grad,), own_b, other_b, weight, 1)
            if stage == 0:
                return (finish_layer(*pieces), grad), empty
            pieces = backward_layer(scalar_core, pieces, own_a, other_a, weight, 0)
            return (pieces[0], grad), finish_layer(*pieces)

        def rest(operands, grads=grads):
            return grads, empty

        grads, leaving = lax.cond(
            chip == stage, turn, rest, (arriving, own_a, other_a, own_b, other_b, weight)
        )
        if stage > 0:
            arriving = hop(leaving, stage, -1)
        if stage == chips - 1:
            own = jnp.where(core == 0, own_a, own_b)
            other = jnp.where(core == 0, other_a, other_b)
            own, other, leaving = lax.optimization_barrier((own, other, leaving))
            full = halves(core, own, other).astype(f32)
            mean = jnp.mean(full * full, axis=-1, keepdims=True)
            full = (full * lax.rsqrt(mean + EPSILON)).astype(bf16)
            taken = spread(full)
            parts = gram_halves(taken, live, odd)
            arriving, parts = lax.optimization_barrier((arriving, parts))
        elif stage == chips - 2:
            grads, parts = lax.optimization_barrier((grads, parts))
            inverses = sum_and_invert(*parts, counted, odd)
            pre_inputs = gather_back(apply_blocks(taken, inverses))
            arriving, pre_inputs = lax.optimization_barrier((arriving, pre_inputs))

    grad_a, grad_b = grads
    own = jnp.where(core == 0, grad_a, grad_b)
    other = swap_cores(jnp.where(core == 0, grad_b, grad_a))
    taken = spread(halves(core, own, other))
    inverses = sum_and_invert(*gram_halves(taken, live, odd), counted, odd)
    pre_grads = gather_back(apply_blocks(taken, inverses))
    return (pre_inputs[None], pre_grads[None])


def solution(mesh):
    in_specs = (P("dp", None), P("dp", None), P("section", "dp", None), P("dp"))
    out_specs = (P("section", "dp", None), P("section", "dp", None))
    return jax.shard_map(
        all_stages, mesh=mesh, in_specs=in_specs, out_specs=out_specs, check_vma=False
    )
```

```python
import functools

import jax
import jax.numpy as jnp
from jax import lax
from jax.experimental import pallas as pl
from jax.experimental.pallas import tpu as pltpu
from jax.sharding import PartitionSpec as P


BLOCK = 160
EPSILON = 1e-05
DAMPING = 0.1
LANES = 128
TILE = 640
ROWS = 640

f32 = jnp.float32
bf16 = jnp.bfloat16


def row_factor(own, other, width):
    total = jnp.sum(own * own, axis=-1, keepdims=True)
    total = total + jnp.sum(other * other, axis=-1, keepdims=True)
    return lax.rsqrt(total / width + EPSILON)


def forward_kernel(core_ref, own_ref, other_ref, wown_ref, wother_ref, out_ref, aown, aother):
    step = pl.program_id(0)
    half = own_ref.shape[1]

    @pl.when(step == 0)
    def _():
        own = own_ref[...].astype(f32)
        other = other_ref[...].astype(f32)
        factor = row_factor(own, other, 2 * half)
        aown[...] = (own * factor).astype(bf16)
        aother[...] = (other * factor).astype(bf16)

    result = jnp.dot(aown[...], wown_ref[...], preferred_element_type=f32)
    result = result + jnp.dot(aother[...], wother_ref[...], preferred_element_type=f32)
    columns = pl.ds(pl.multiple_of(step * TILE, TILE), TILE)
    out_ref[...] = (own_ref[:, columns].astype(f32) + result).astype(bf16)


def forward_layer(core, own, other, weight, which):
    rows, half = own.shape
    steps = half // TILE
    whole = pl.BlockSpec((rows, half), lambda i, c: (0, 0))
    return pl.pallas_call(
        forward_kernel,
        out_shape=jax.ShapeDtypeStruct((rows, half), bf16),
        grid_spec=pltpu.PrefetchScalarGridSpec(
            num_scalar_prefetch=1,
            grid=(steps,),
            in_specs=[
                whole,
                whole,
                pl.BlockSpec((half, TILE), lambda i, c: (c[0], which * steps + i)),
                pl.BlockSpec((half, TILE), lambda i, c: (1 - c[0], which * steps + i)),
            ],
            out_specs=pl.BlockSpec((rows, TILE), lambda i, c: (0, i)),
            scratch_shapes=[pltpu.VMEM((rows, half), bf16), pltpu.VMEM((rows, half), bf16)],
        ),
        cost_estimate=pl.CostEstimate(
            flops=4 * rows * half * half, bytes_accessed=4 * half * half, transcendentals=0
        ),
    )(core, own, other, weight, weight)


def finish(grad, keep, arrived, own):
    half = own.shape[1]
    mine, theirs = keep[:, half + LANES :], arrived[:, half:].astype(f32)
    mean = jnp.sum(mine + theirs, axis=-1, keepdims=True) / (2 * half)
    factor = keep[:, half : half + 1]
    back = keep[:, :half] + arrived[:, :half].astype(f32)
    through = factor * (back - own.astype(f32) * factor * mean)
    return (grad.astype(f32) + through).astype(bf16)


def finish_kernel(grad_ref, keep_ref, arrived_ref, own_ref, out_ref):
    out_ref[...] = finish(grad_ref[...], keep_ref[...], arrived_ref[...], own_ref[...])


def finish_layer(grad, keep, arrived, own):
    rows, half = own.shape
    whole = pl.BlockSpec(memory_space=pltpu.VMEM)
    return pl.pallas_call(
        finish_kernel,
        out_shape=jax.ShapeDtypeStruct((rows, half), bf16),
        in_specs=[whole] * 4,
        out_specs=whole,
        cost_estimate=pl.CostEstimate(
            flops=8 * rows * half, bytes_accessed=16 * rows * half, transcendentals=0
        ),
    )(grad, keep, arrived, own)


def backward_kernel(fused, core_ref, *refs):
    if fused:
        before, refs = refs[:4], refs[4:]
        own_ref, other_ref, weight_ref, send_ref, keep_ref, grad_ref = refs
    else:
        grad_ref, own_ref, other_ref, weight_ref, send_ref, keep_ref = refs
    step = pl.program_id(0)
    rows, half = own_ref.shape
    steps = half // ROWS
    factor_at, product_at = slice(half, half + LANES), slice(half + LANES, half + 2 * LANES)

    @pl.when(step == 0)
    def _():
        if fused:
            grad_ref[...] = finish(*[ref[...] for ref in before])
        own = own_ref[...].astype(f32)
        other = other_ref[...].astype(f32)
        keep_ref[:, factor_at] = jnp.broadcast_to(row_factor(own, other, 2 * half), (rows, LANES))
        keep_ref[:, product_at] = jnp.zeros((rows, LANES), f32)

    part = lax.dot_general(
        grad_ref[...], weight_ref[...], (((1,), (1,)), ((), ())), preferred_element_type=f32
    )

    def along(hidden_ref, columns):
        product = part * hidden_ref[:, columns].astype(f32)
        folded = product[:, :LANES]
        for k in range(1, ROWS // LANES):
            folded = folded + product[:, k * LANES : (k + 1) * LANES]
        keep_ref[:, product_at] += folded * keep_ref[:, factor_at]

    @pl.when(step < steps)
    def _():
        columns = pl.ds(pl.multiple_of(step * ROWS, LANES), ROWS)
        send_ref[:, columns] = part.astype(bf16)
        along(other_ref, columns)

    @pl.when(step >= steps)
    def _():
        columns = pl.ds(pl.multiple_of((step - steps) * ROWS, LANES), ROWS)
        keep_ref[:, columns] = part
        along(own_ref, columns)

    @pl.when(step == 2 * steps - 1)
    def _():
        send_ref[:, half:] = keep_ref[:, product_at].astype(bf16)


def backward_layer(core, before, own, other, weight, which):
    rows, half = own.shape
    steps = half // ROWS
    fused = len(before) > 1

    def whole(extra=0):
        return pl.BlockSpec((rows, half + extra), lambda i, c: (0, 0))

    def place(i, c):
        return (jnp.where(i < steps, (1 - c[0]) * steps + i, c[0] * steps + i - steps), which)

    out_shape = [
        jax.ShapeDtypeStruct((rows, half + LANES), bf16),
        jax.ShapeDtypeStruct((rows, half + 2 * LANES), f32),
    ]
    first = [whole(), whole(2 * LANES), whole(LANES), whole()] if fused else [whole()]
    results = pl.pallas_call(
        functools.partial(backward_kernel, fused),
        out_shape=out_shape + [jax.ShapeDtypeStruct((rows, half), bf16)] * fused,
        grid_spec=pltpu.PrefetchScalarGridSpec(
            num_scalar_prefetch=1,
            grid=(2 * steps,),
            in_specs=first + [whole(), whole(), pl.BlockSpec((ROWS, half), place)],
            out_specs=[whole(LANES), whole(2 * LANES)] + [whole()] * fused,
        ),
        cost_estimate=pl.CostEstimate(
            flops=4 * rows * half * half, bytes_accessed=4 * half * half, transcendentals=0
        ),
    )(core, *before, own, other, weight)
    send, keep = results[:2]
    grad = results[2] if fused else before[0]
    return (grad, keep, swap_cores(send), own)


def inverse_kernel(first_ref, second_ref, third_ref, fourth_ref, count_ref, out_ref):
    order = out_ref.shape[0]
    rows = lax.broadcasted_iota(jnp.int32, (order, order), 0)
    columns = lax.broadcasted_iota(jnp.int32, (order, order), 1)
    row, column = columns[:1], rows[:, :1]
    block = (first_ref[...] + second_ref[...]) + (third_ref[...] + fourth_ref[...])
    block = block / count_ref[0]
    block = block + jnp.where(rows == columns, DAMPING, 0.0)
    for k in range(0, order, 2):
        n = k + 1
        a, b, c = block[k : k + 1, k : k + 1], block[k : k + 1, n : n + 1], block[n : n + 1, n : n + 1]
        scale = 1.0 / (a * c - b * b)
        row_k = jnp.where(row == k, -1.0, jnp.where(row == n, 0.0, block[k : k + 1, :]))
        row_n = jnp.where(row == n, -1.0, jnp.where(row == k, 0.0, block[n : n + 1, :]))
        column_k = jnp.where(column == k, -1.0, jnp.where(column == n, 0.0, block[:, k : k + 1]))
        column_n = jnp.where(column == n, -1.0, jnp.where(column == k, 0.0, block[:, n : n + 1]))
        solved_k = (c * row_k - b * row_n) * scale
        solved_n = (a * row_n - b * row_k) * scale
        outside = (rows // 2 != k // 2) & (columns // 2 != k // 2)
        block = jnp.where(outside, block, 0.0) - column_k * solved_k - column_n * solved_n
    out_ref[...] = (-block).astype(bf16)


def invert_block(parts, counted):
    order = parts[0].shape[0]
    return pl.pallas_call(
        inverse_kernel,
        out_shape=jax.ShapeDtypeStruct((order, order), bf16),
        in_specs=[
            *[pl.BlockSpec(memory_space=pltpu.VMEM)] * 4,
            pl.BlockSpec(memory_space=pltpu.SMEM),
        ],
        out_specs=pl.BlockSpec(memory_space=pltpu.VMEM),
    )(*parts, counted)


def swap_cores(array):
    count = lax.axis_size("section")
    return lax.ppermute(array, "section", [(i, i ^ 1) for i in range(count)])


def hop(array, source, by):
    pairs = [(2 * source + core, 2 * (source + by) + core) for core in range(2)]
    return lax.ppermute(array, "section", pairs)


GROUP = 8


def groups_near(count):
    return [list(range(base, base + GROUP)) for base in range(0, count, GROUP)]


def swap_groups(array, apart):
    count = lax.axis_size("dp")
    pairs = [(i, (i // GROUP ^ apart) * GROUP + i % GROUP) for i in range(count)]
    return lax.ppermute(array, "dp", pairs)


def halves(core, own, other):
    first = jnp.where(core == 0, own, other)
    second = jnp.where(core == 0, other, own)
    return jnp.concatenate([first, second], axis=1)


def spread(values):
    lines = groups_near(lax.axis_size("dp"))
    return lax.all_to_all(
        values, "dp", split_axis=1, concat_axis=0, axis_index_groups=lines, tiled=True
    )


def gather_back(values):
    lines = groups_near(lax.axis_size("dp"))
    return lax.all_to_all(
        values, "dp", split_axis=0, concat_axis=1, axis_index_groups=lines, tiled=True
    )


def gram_halves(taken, live, odd):
    masked = jnp.where(live, taken, jnp.zeros((), bf16))
    grams = []
    for b in range(2):
        part = masked[:, b * BLOCK : (b + 1) * BLOCK]
        grams.append(
            lax.dot_general(part, part, (((0,), (0,)), ((), ())), preferred_element_type=f32)
        )
    mine = jnp.where(odd, grams[1], grams[0])
    theirs = jnp.where(odd, grams[0], grams[1])
    return mine, theirs


def sum_and_invert(mine, theirs, counted, odd):
    parts = (mine, swap_groups(theirs, 1), swap_groups(mine, 2), swap_groups(theirs, 3))
    inverse = invert_block(parts, counted)
    other = swap_groups(inverse, 1)
    return jnp.where(odd, other, inverse), jnp.where(odd, inverse, other)


def apply_blocks(taken, inverses):
    results = [
        jnp.dot(
            taken[:, b * BLOCK : (b + 1) * BLOCK], inverse, preferred_element_type=f32
        ).astype(bf16)
        for b, inverse in enumerate(inverses)
    ]
    return jnp.concatenate(results, axis=1)


def all_stages(inputs, cotangent, weights, lengths):
    section = lax.axis_index("section")
    chip, core = section // 2, section % 2
    chips = lax.axis_size("section") // 2
    tokens, width = inputs.shape
    half = width // 2
    batch_rows = tokens // lengths.shape[0]
    scalar_core = core.reshape(1).astype(jnp.int32)

    local = weights[0]
    mine = jnp.where(core == 0, local[:, :half], local[:, half:])
    theirs = jnp.where(core == 0, local[:, half:], local[:, :half])
    swapped = swap_cores(theirs)
    paired = halves(core, mine, swapped)
    weight = lax.all_gather(paired, "dp", axis=0, tiled=True)

    all_lengths = lax.all_gather(lengths, "dp", axis=0)
    alive = jnp.clip(all_lengths, 0, batch_rows)
    counted = jnp.sum(alive).astype(f32).reshape(1)
    near = lax.axis_index("dp") // GROUP
    odd = near % 2 == 1
    line = lax.dynamic_index_in_dim(all_lengths.reshape(4, GROUP, -1), near, 0, keepdims=False)
    live = (jnp.arange(batch_rows)[None, :] < line.reshape(-1, 1)).reshape(-1, 1)

    def own_half(array):
        return jnp.where(core == 0, array[:, :half], array[:, half:])

    def other_half(array):
        return jnp.where(core == 0, array[:, half:], array[:, :half])

    first_own = own_half(inputs)
    first_own, counted, live = lax.optimization_barrier((first_own, counted, live))
    empty = jnp.zeros((tokens, half), bf16)
    kept = (empty, empty, empty, empty)
    arriving = first_own
    for stage in range(chips):
        last = stage == chips - 1

        def turn(operands, stage=stage, last=last):
            own, weight = operands
            other = other_half(inputs) if stage == 0 else swap_cores(own)
            second = forward_layer(scalar_core, own, other, weight, 0)
            second_other = swap_cores(second)
            if last:
                leaving = empty
            else:
                leaving = forward_layer(scalar_core, second, second_other, weight, 1)
            return (own, other, second, second_other), leaving

        def rest(operands, kept=kept):
            return kept, empty

        kept, leaving = lax.cond(chip == stage, turn, rest, (arriving, weight))
        if not last:
            arriving = hop(leaving, stage, 1)

    own_a, other_a, own_b, other_b = kept
    grads = (empty, empty)
    arriving = own_half(cotangent)
    pre_inputs = None
    taken = None
    for stage in range(chips - 1, -1, -1):

        def turn(operands, stage=stage):
            grad, own_a, other_a, own_b, other_b, weight = operands
            pieces = backward_layer(scalar_core, (grad,), own_b, other_b, weight, 1)
            if stage == 0:
                return (finish_layer(*pieces), grad), empty
            pieces = backward_layer(scalar_core, pieces, own_a, other_a, weight, 0)
            return (pieces[0], grad), finish_layer(*pieces)

        def rest(operands, grads=grads):
            return grads, empty

        grads, leaving = lax.cond(
            chip == stage, turn, rest, (arriving, own_a, other_a, own_b, other_b, weight)
        )
        if stage > 0:
            arriving = hop(leaving, stage, -1)
        if stage == chips - 1:
            own = jnp.where(core == 0, own_a, own_b)
            other = jnp.where(core == 0, other_a, other_b)
            own, other, leaving = lax.optimization_barrier((own, other, leaving))
            full = halves(core, own, other).astype(f32)
            mean = jnp.mean(full * full, axis=-1, keepdims=True)
            full = (full * lax.rsqrt(mean + EPSILON)).astype(bf16)
            taken = spread(full)
            parts = gram_halves(taken, live, odd)
            arriving, parts = lax.optimization_barrier((arriving, parts))
        elif stage == chips - 2:
            grads, parts = lax.optimization_barrier((grads, parts))
            inverses = sum_and_invert(*parts, counted, odd)
            pre_inputs = gather_back(apply_blocks(taken, inverses))
            arriving, pre_inputs = lax.optimization_barrier((arriving, pre_inputs))

    grad_a, grad_b = grads
    own = jnp.where(core == 0, grad_a, grad_b)
    other = swap_cores(jnp.where(core == 0, grad_b, grad_a))
    taken = spread(halves(core, own, other))
    inverses = sum_and_invert(*gram_halves(taken, live, odd), counted, odd)
    pre_grads = gather_back(apply_blocks(taken, inverses))
    return (pre_inputs[None], pre_grads[None])


def solution(mesh):
    in_specs = (P("dp", None), P("dp", None), P("section", "dp", None), P("dp"))
    out_specs = (P("section", "dp", None), P("section", "dp", None))
    return jax.shard_map(
        all_stages, mesh=mesh, in_specs=in_specs, out_specs=out_specs, check_vma=False
    )
```

```python
import functools

import jax
import jax.numpy as jnp
from jax import lax
from jax.experimental import pallas as pl
from jax.experimental.pallas import tpu as pltpu
from jax.sharding import PartitionSpec as P


BLOCK = 160
EPSILON = 1e-05
DAMPING = 0.1
LANES = 128
TILE = 640
ROWS = 640

f32 = jnp.float32
bf16 = jnp.bfloat16


def row_factor(own, other, width):
    total = jnp.sum(own * own, axis=-1, keepdims=True)
    total = total + jnp.sum(other * other, axis=-1, keepdims=True)
    return lax.rsqrt(total / width + EPSILON)


def forward_kernel(core_ref, own_ref, other_ref, wown_ref, wother_ref, out_ref, aown, aother):
    step = pl.program_id(0)
    half = own_ref.shape[1]

    @pl.when(step == 0)
    def _():
        own = own_ref[...].astype(f32)
        other = other_ref[...].astype(f32)
        factor = row_factor(own, other, 2 * half)
        aown[...] = (own * factor).astype(bf16)
        aother[...] = (other * factor).astype(bf16)

    result = jnp.dot(aown[...], wown_ref[...], preferred_element_type=f32)
    result = result + jnp.dot(aother[...], wother_ref[...], preferred_element_type=f32)
    columns = pl.ds(pl.multiple_of(step * TILE, TILE), TILE)
    out_ref[...] = (own_ref[:, columns].astype(f32) + result).astype(bf16)


def forward_layer(core, own, other, weight, which):
    rows, half = own.shape
    steps = half // TILE
    whole = pl.BlockSpec((rows, half), lambda i, c: (0, 0))

    def at(c):
        return 1 - c[0] if which else c[0]

    return pl.pallas_call(
        forward_kernel,
        out_shape=jax.ShapeDtypeStruct((rows, half), bf16),
        grid_spec=pltpu.PrefetchScalarGridSpec(
            num_scalar_prefetch=1,
            grid=(steps,),
            in_specs=[
                whole,
                whole,
                pl.BlockSpec((half, TILE), lambda i, c: (c[0], at(c) * steps + i)),
                pl.BlockSpec((half, TILE), lambda i, c: (1 - c[0], at(c) * steps + i)),
            ],
            out_specs=pl.BlockSpec((rows, TILE), lambda i, c: (0, i)),
            scratch_shapes=[pltpu.VMEM((rows, half), bf16), pltpu.VMEM((rows, half), bf16)],
        ),
        cost_estimate=pl.CostEstimate(
            flops=4 * rows * half * half, bytes_accessed=4 * half * half, transcendentals=0
        ),
    )(core, own, other, weight, weight)


def finish(grad, keep, arrived, own):
    half = own.shape[1]
    mine, theirs = keep[:, half + LANES :], arrived[:, half:].astype(f32)
    mean = jnp.sum(mine + theirs, axis=-1, keepdims=True) / (2 * half)
    factor = keep[:, half : half + 1]
    back = keep[:, :half] + arrived[:, :half].astype(f32)
    through = factor * (back - own.astype(f32) * factor * mean)
    return (grad.astype(f32) + through).astype(bf16)


def finish_kernel(grad_ref, keep_ref, arrived_ref, own_ref, out_ref):
    out_ref[...] = finish(grad_ref[...], keep_ref[...], arrived_ref[...], own_ref[...])


def finish_layer(grad, keep, arrived, own):
    rows, half = own.shape
    whole = pl.BlockSpec(memory_space=pltpu.VMEM)
    return pl.pallas_call(
        finish_kernel,
        out_shape=jax.ShapeDtypeStruct((rows, half), bf16),
        in_specs=[whole] * 4,
        out_specs=whole,
        cost_estimate=pl.CostEstimate(
            flops=8 * rows * half, bytes_accessed=16 * rows * half, transcendentals=0
        ),
    )(grad, keep, arrived, own)


def backward_kernel(fused, core_ref, *refs):
    if fused:
        before, refs = refs[:4], refs[4:]
        own_ref, other_ref, weight_ref, send_ref, keep_ref, grad_ref = refs
    else:
        grad_ref, own_ref, other_ref, weight_ref, send_ref, keep_ref = refs
    step = pl.program_id(0)
    rows, half = own_ref.shape
    steps = half // ROWS
    factor_at, product_at = slice(half, half + LANES), slice(half + LANES, half + 2 * LANES)

    @pl.when(step == 0)
    def _():
        if fused:
            grad_ref[...] = finish(*[ref[...] for ref in before])
        own = own_ref[...].astype(f32)
        other = other_ref[...].astype(f32)
        keep_ref[:, factor_at] = jnp.broadcast_to(row_factor(own, other, 2 * half), (rows, LANES))
        keep_ref[:, product_at] = jnp.zeros((rows, LANES), f32)

    part = lax.dot_general(
        grad_ref[...], weight_ref[...], (((1,), (1,)), ((), ())), preferred_element_type=f32
    )

    def along(hidden_ref, columns):
        product = part * hidden_ref[:, columns].astype(f32)
        folded = product[:, :LANES]
        for k in range(1, ROWS // LANES):
            folded = folded + product[:, k * LANES : (k + 1) * LANES]
        keep_ref[:, product_at] += folded * keep_ref[:, factor_at]

    @pl.when(step < steps)
    def _():
        columns = pl.ds(pl.multiple_of(step * ROWS, LANES), ROWS)
        send_ref[:, columns] = part.astype(bf16)
        along(other_ref, columns)

    @pl.when(step >= steps)
    def _():
        columns = pl.ds(pl.multiple_of((step - steps) * ROWS, LANES), ROWS)
        keep_ref[:, columns] = part
        along(own_ref, columns)

    @pl.when(step == 2 * steps - 1)
    def _():
        send_ref[:, half:] = keep_ref[:, product_at].astype(bf16)


def backward_layer(core, before, own, other, weight, which):
    rows, half = own.shape
    steps = half // ROWS
    fused = len(before) > 1

    def whole(extra=0):
        return pl.BlockSpec((rows, half + extra), lambda i, c: (0, 0))

    def place(i, c):
        return (jnp.where(i < steps, (1 - c[0]) * steps + i, c[0] * steps + i - steps), 1 - c[0] if which else c[0])

    out_shape = [
        jax.ShapeDtypeStruct((rows, half + LANES), bf16),
        jax.ShapeDtypeStruct((rows, half + 2 * LANES), f32),
    ]
    first = [whole(), whole(2 * LANES), whole(LANES), whole()] if fused else [whole()]
    results = pl.pallas_call(
        functools.partial(backward_kernel, fused),
        out_shape=out_shape + [jax.ShapeDtypeStruct((rows, half), bf16)] * fused,
        grid_spec=pltpu.PrefetchScalarGridSpec(
            num_scalar_prefetch=1,
            grid=(2 * steps,),
            in_specs=first + [whole(), whole(), pl.BlockSpec((ROWS, half), place)],
            out_specs=[whole(LANES), whole(2 * LANES)] + [whole()] * fused,
        ),
        cost_estimate=pl.CostEstimate(
            flops=4 * rows * half * half, bytes_accessed=4 * half * half, transcendentals=0
        ),
    )(core, *before, own, other, weight)
    send, keep = results[:2]
    grad = results[2] if fused else before[0]
    return (grad, keep, swap_cores(send), own)


PANEL = 32


def inverse_kernel(first_ref, second_ref, third_ref, fourth_ref, count_ref, out_ref, work):
    order = out_ref.shape[0]
    rows = lax.broadcasted_iota(jnp.int32, (order, order), 0)
    columns = lax.broadcasted_iota(jnp.int32, (order, order), 1)
    row, column = columns[:1], rows[:, :1]
    total = (first_ref[...] + second_ref[...]) + (third_ref[...] + fourth_ref[...])
    work[...] = total / count_ref[0] + jnp.where(rows == columns, DAMPING, 0.0)

    def panel(_, carry):
        block = work[...]
        for k in range(0, PANEL, 2):
            n = k + 1
            a, b = block[k : k + 1, k : k + 1], block[k : k + 1, n : n + 1]
            c = block[n : n + 1, n : n + 1]
            scale = 1.0 / (a * c - b * b)
            row_k = jnp.where(row == k, -1.0, jnp.where(row == n, 0.0, block[k : k + 1, :]))
            row_n = jnp.where(row == n, -1.0, jnp.where(row == k, 0.0, block[n : n + 1, :]))
            column_k = jnp.where(column == k, -1.0, jnp.where(column == n, 0.0, block[:, k : k + 1]))
            column_n = jnp.where(column == n, -1.0, jnp.where(column == k, 0.0, block[:, n : n + 1]))
            solved_k = (c * row_k - b * row_n) * scale
            solved_n = (a * row_n - b * row_k) * scale
            outside = (rows // 2 != k // 2) & (columns // 2 != k // 2)
            block = jnp.where(outside, block, 0.0) - column_k * solved_k - column_n * solved_n
        rest = order - PANEL
        work[:rest, :rest] = block[PANEL:, PANEL:]
        work[:rest, rest:] = block[PANEL:, :PANEL]
        work[rest:, :rest] = block[:PANEL, PANEL:]
        work[rest:, rest:] = block[:PANEL, :PANEL]
        return carry

    lax.fori_loop(0, order // PANEL, panel, 0)
    out_ref[...] = (-work[...]).astype(bf16)


def invert_block(parts, counted):
    order = parts[0].shape[0]
    return pl.pallas_call(
        inverse_kernel,
        out_shape=jax.ShapeDtypeStruct((order, order), bf16),
        in_specs=[
            *[pl.BlockSpec(memory_space=pltpu.VMEM)] * 4,
            pl.BlockSpec(memory_space=pltpu.SMEM),
        ],
        out_specs=pl.BlockSpec(memory_space=pltpu.VMEM),
        scratch_shapes=[pltpu.VMEM((order, order), f32)],
    )(*parts, counted)


def swap_cores(array):
    count = lax.axis_size("section")
    return lax.ppermute(array, "section", [(i, i ^ 1) for i in range(count)])


def hop(array, source, by):
    pairs = [(2 * source + core, 2 * (source + by) + core) for core in range(2)]
    return lax.ppermute(array, "section", pairs)


GROUP = 8


def groups_near(count):
    return [list(range(base, base + GROUP)) for base in range(0, count, GROUP)]


def swap_groups(array, apart):
    count = lax.axis_size("dp")
    pairs = [(i, (i // GROUP ^ apart) * GROUP + i % GROUP) for i in range(count)]
    return lax.ppermute(array, "dp", pairs)


def halves(core, own, other):
    first = jnp.where(core == 0, own, other)
    second = jnp.where(core == 0, other, own)
    return jnp.concatenate([first, second], axis=1)


def spread(values):
    lines = groups_near(lax.axis_size("dp"))
    return lax.all_to_all(
        values, "dp", split_axis=1, concat_axis=0, axis_index_groups=lines, tiled=True
    )


def gather_back(values):
    lines = groups_near(lax.axis_size("dp"))
    return lax.all_to_all(
        values, "dp", split_axis=0, concat_axis=1, axis_index_groups=lines, tiled=True
    )


def gram_halves(taken, live, odd):
    masked = jnp.where(live, taken, jnp.zeros((), bf16))
    grams = []
    for b in range(2):
        part = masked[:, b * BLOCK : (b + 1) * BLOCK]
        grams.append(
            lax.dot_general(part, part, (((0,), (0,)), ((), ())), preferred_element_type=f32)
        )
    mine = jnp.where(odd, grams[1], grams[0])
    theirs = jnp.where(odd, grams[0], grams[1])
    return mine, theirs


def share_parts(mine, theirs):
    return (mine, swap_groups(theirs, 1), swap_groups(mine, 2), swap_groups(theirs, 3))


def invert_all(parts, counted, odd):
    inverse = invert_block(parts, counted)
    other = swap_groups(inverse, 1)
    return jnp.where(odd, other, inverse), jnp.where(odd, inverse, other)


def apply_blocks(taken, inverses):
    results = [
        jnp.dot(
            taken[:, b * BLOCK : (b + 1) * BLOCK], inverse, preferred_element_type=f32
        ).astype(bf16)
        for b, inverse in enumerate(inverses)
    ]
    return jnp.concatenate(results, axis=1)


def all_stages(inputs, cotangent, weights, lengths):
    section = lax.axis_index("section")
    chip, core = section // 2, section % 2
    chips = lax.axis_size("section") // 2
    tokens, width = inputs.shape
    half = width // 2
    batch_rows = tokens // lengths.shape[0]
    scalar_core = core.reshape(1).astype(jnp.int32)

    local = weights[0]
    mine = jnp.where(core == 0, local[:, :half], local[:, half:])
    theirs = jnp.where(core == 0, local[:, half:], local[:, :half])
    swapped = swap_cores(theirs)
    paired = jnp.concatenate([mine, swapped], axis=1)
    weight = lax.all_gather(paired, "dp", axis=0, tiled=True)

    all_lengths = lax.all_gather(lengths, "dp", axis=0)
    alive = jnp.clip(all_lengths, 0, batch_rows)
    counted = jnp.sum(alive).astype(f32).reshape(1)
    near = lax.axis_index("dp") // GROUP
    odd = near % 2 == 1
    line = lax.dynamic_index_in_dim(all_lengths.reshape(4, GROUP, -1), near, 0, keepdims=False)
    live = (jnp.arange(batch_rows)[None, :] < line.reshape(-1, 1)).reshape(-1, 1)

    def own_half(array):
        return jnp.where(core == 0, array[:, :half], array[:, half:])

    def other_half(array):
        return jnp.where(core == 0, array[:, half:], array[:, :half])

    first_own = own_half(inputs)
    first_own, counted, live = lax.optimization_barrier((first_own, counted, live))
    empty = jnp.zeros((tokens, half), bf16)
    kept = (empty, empty, empty, empty)
    arriving = first_own
    for stage in range(chips):
        last = stage == chips - 1

        def turn(operands, stage=stage, last=last):
            own, weight = operands
            other = other_half(inputs) if stage == 0 else swap_cores(own)
            second = forward_layer(scalar_core, own, other, weight, 0)
            second_other = swap_cores(second)
            if last:
                leaving = empty
            else:
                leaving = forward_layer(scalar_core, second, second_other, weight, 1)
            return (own, other, second, second_other), leaving

        def rest(operands, kept=kept):
            return kept, empty

        kept, leaving = lax.cond(chip == stage, turn, rest, (arriving, weight))
        if not last:
            arriving = hop(leaving, stage, 1)

    own_a, other_a, own_b, other_b = kept
    grads = (empty, empty)
    arriving = own_half(cotangent)
    pre_inputs = None
    taken = None
    for stage in range(chips - 1, -1, -1):

        def turn(operands, stage=stage):
            grad, own_a, other_a, own_b, other_b, weight = operands
            pieces = backward_layer(scalar_core, (grad,), own_b, other_b, weight, 1)
            if stage == 0:
                return (finish_layer(*pieces), grad), empty
            pieces = backward_layer(scalar_core, pieces, own_a, other_a, weight, 0)
            return (pieces[0], grad), finish_layer(*pieces)

        def rest(operands, grads=grads):
            return grads, empty

        grads, leaving = lax.cond(
            chip == stage, turn, rest, (arriving, own_a, other_a, own_b, other_b, weight)
        )
        if stage > 0:
            arriving = hop(leaving, stage, -1)
        if stage == chips - 1:
            own = jnp.where(core == 0, own_a, own_b)
            other = jnp.where(core == 0, other_a, other_b)
            own, other, leaving = lax.optimization_barrier((own, other, leaving))
            full = halves(core, own, other).astype(f32)
            mean = jnp.mean(full * full, axis=-1, keepdims=True)
            full = (full * lax.rsqrt(mean + EPSILON)).astype(bf16)
            taken = spread(full)
            parts = share_parts(*gram_halves(taken, live, odd))
            arriving, parts = lax.optimization_barrier((arriving, parts))
        elif stage == chips - 2:
            grads, parts = lax.optimization_barrier((grads, parts))
            inverses = invert_all(parts, counted, odd)
            pre_inputs = gather_back(apply_blocks(taken, inverses))
            arriving, pre_inputs = lax.optimization_barrier((arriving, pre_inputs))

    grad_a, grad_b = grads
    own = jnp.where(core == 0, grad_a, grad_b)
    other = swap_cores(jnp.where(core == 0, grad_b, grad_a))
    taken = spread(halves(core, own, other))
    inverses = invert_all(share_parts(*gram_halves(taken, live, odd)), counted, odd)
    pre_grads = gather_back(apply_blocks(taken, inverses))
    return (pre_inputs[None], pre_grads[None])


def solution(mesh):
    in_specs = (P("dp", None), P("dp", None), P("section", "dp", None), P("dp"))
    out_specs = (P("section", "dp", None), P("section", "dp", None))
    return jax.shard_map(
        all_stages, mesh=mesh, in_specs=in_specs, out_specs=out_specs, check_vma=False
    )
```

```python
import functools

import jax
import jax.numpy as jnp
from jax import lax
from jax.experimental import pallas as pl
from jax.experimental.pallas import tpu as pltpu
from jax.sharding import PartitionSpec as P


BLOCK = 160
EPSILON = 1e-05
DAMPING = 0.1
LANES = 128
GRANT = 52 * 1024 * 1024
TILE = 640
ROWS = 640

f32 = jnp.float32
bf16 = jnp.bfloat16


def row_factor(own, other, width):
    total = jnp.sum(own * own, axis=-1, keepdims=True)
    total = total + jnp.sum(other * other, axis=-1, keepdims=True)
    return lax.rsqrt(total / width + EPSILON)


def forward_kernel(core_ref, own_ref, other_ref, wown_ref, wother_ref, out_ref, aown, aother):
    step = pl.program_id(0)
    half = own_ref.shape[1]

    @pl.when(step == 0)
    def _():
        own = own_ref[...].astype(f32)
        other = other_ref[...].astype(f32)
        factor = row_factor(own, other, 2 * half)
        aown[...] = (own * factor).astype(bf16)
        aother[...] = (other * factor).astype(bf16)

    result = jnp.dot(aown[...], wown_ref[...], preferred_element_type=f32)
    result = result + jnp.dot(aother[...], wother_ref[...], preferred_element_type=f32)
    columns = pl.ds(pl.multiple_of(step * TILE, TILE), TILE)
    out_ref[...] = (own_ref[:, columns].astype(f32) + result).astype(bf16)


def forward_layer(core, own, other, weight, which):
    rows, half = own.shape
    steps = half // TILE
    whole = pl.BlockSpec((rows, half), lambda i, c: (0, 0))

    def at(c):
        return 1 - c[0] if which else c[0]

    return pl.pallas_call(
        forward_kernel,
        out_shape=jax.ShapeDtypeStruct((rows, half), bf16),
        grid_spec=pltpu.PrefetchScalarGridSpec(
            num_scalar_prefetch=1,
            grid=(steps,),
            in_specs=[
                whole,
                whole,
                pl.BlockSpec((half, TILE), lambda i, c: (c[0], at(c) * steps + i)),
                pl.BlockSpec((half, TILE), lambda i, c: (1 - c[0], at(c) * steps + i)),
            ],
            out_specs=pl.BlockSpec((rows, TILE), lambda i, c: (0, i)),
            scratch_shapes=[pltpu.VMEM((rows, half), bf16), pltpu.VMEM((rows, half), bf16)],
        ),
        compiler_params=pltpu.CompilerParams(vmem_limit_bytes=GRANT),
        cost_estimate=pl.CostEstimate(
            flops=4 * rows * half * half, bytes_accessed=4 * half * half, transcendentals=0
        ),
    )(core, own, other, weight, weight)


def finish(grad, keep, arrived, own):
    half = own.shape[1]
    mine, theirs = keep[:, half + LANES :], arrived[:, half:].astype(f32)
    mean = jnp.sum(mine + theirs, axis=-1, keepdims=True) / (2 * half)
    factor = keep[:, half : half + 1]
    back = keep[:, :half] + arrived[:, :half].astype(f32)
    through = factor * (back - own.astype(f32) * factor * mean)
    return (grad.astype(f32) + through).astype(bf16)


def finish_kernel(grad_ref, keep_ref, arrived_ref, own_ref, out_ref):
    out_ref[...] = finish(grad_ref[...], keep_ref[...], arrived_ref[...], own_ref[...])


def finish_layer(grad, keep, arrived, own):
    rows, half = own.shape
    whole = pl.BlockSpec(memory_space=pltpu.VMEM)
    return pl.pallas_call(
        finish_kernel,
        out_shape=jax.ShapeDtypeStruct((rows, half), bf16),
        in_specs=[whole] * 4,
        out_specs=whole,
        compiler_params=pltpu.CompilerParams(vmem_limit_bytes=GRANT),
        cost_estimate=pl.CostEstimate(
            flops=8 * rows * half, bytes_accessed=16 * rows * half, transcendentals=0
        ),
    )(grad, keep, arrived, own)


def backward_kernel(fused, core_ref, *refs):
    if fused:
        before, refs = refs[:4], refs[4:]
        own_ref, other_ref, weight_ref, send_ref, keep_ref, grad_ref = refs
    else:
        grad_ref, own_ref, other_ref, weight_ref, send_ref, keep_ref = refs
    step = pl.program_id(0)
    rows, half = own_ref.shape
    steps = half // ROWS
    factor_at, product_at = slice(half, half + LANES), slice(half + LANES, half + 2 * LANES)

    @pl.when(step == 0)
    def _():
        if fused:
            grad_ref[...] = finish(*[ref[...] for ref in before])
        own = own_ref[...].astype(f32)
        other = other_ref[...].astype(f32)
        keep_ref[:, factor_at] = jnp.broadcast_to(row_factor(own, other, 2 * half), (rows, LANES))
        keep_ref[:, product_at] = jnp.zeros((rows, LANES), f32)

    part = lax.dot_general(
        grad_ref[...], weight_ref[...], (((1,), (1,)), ((), ())), preferred_element_type=f32
    )

    def along(hidden_ref, columns):
        product = part * hidden_ref[:, columns].astype(f32)
        folded = product[:, :LANES]
        for k in range(1, ROWS // LANES):
            folded = folded + product[:, k * LANES : (k + 1) * LANES]
        keep_ref[:, product_at] += folded * keep_ref[:, factor_at]

    @pl.when(step < steps)
    def _():
        columns = pl.ds(pl.multiple_of(step * ROWS, LANES), ROWS)
        send_ref[:, columns] = part.astype(bf16)
        along(other_ref, columns)

    @pl.when(step >= steps)
    def _():
        columns = pl.ds(pl.multiple_of((step - steps) * ROWS, LANES), ROWS)
        keep_ref[:, columns] = part
        along(own_ref, columns)

    @pl.when(step == 2 * steps - 1)
    def _():
        send_ref[:, half:] = keep_ref[:, product_at].astype(bf16)


def backward_layer(core, before, own, other, weight, which):
    rows, half = own.shape
    steps = half // ROWS
    fused = len(before) > 1

    def whole(extra=0):
        return pl.BlockSpec((rows, half + extra), lambda i, c: (0, 0))

    def place(i, c):
        return (jnp.where(i < steps, (1 - c[0]) * steps + i, c[0] * steps + i - steps), 1 - c[0] if which else c[0])

    out_shape = [
        jax.ShapeDtypeStruct((rows, half + LANES), bf16),
        jax.ShapeDtypeStruct((rows, half + 2 * LANES), f32),
    ]
    first = [whole(), whole(2 * LANES), whole(LANES), whole()] if fused else [whole()]
    results = pl.pallas_call(
        functools.partial(backward_kernel, fused),
        out_shape=out_shape + [jax.ShapeDtypeStruct((rows, half), bf16)] * fused,
        grid_spec=pltpu.PrefetchScalarGridSpec(
            num_scalar_prefetch=1,
            grid=(2 * steps,),
            in_specs=first + [whole(), whole(), pl.BlockSpec((ROWS, half), place)],
            out_specs=[whole(LANES), whole(2 * LANES)] + [whole()] * fused,
        ),
        compiler_params=pltpu.CompilerParams(vmem_limit_bytes=GRANT),
        cost_estimate=pl.CostEstimate(
            flops=4 * rows * half * half, bytes_accessed=4 * half * half, transcendentals=0
        ),
    )(core, *before, own, other, weight)
    send, keep = results[:2]
    grad = results[2] if fused else before[0]
    return (grad, keep, swap_cores(send), own)


PANEL = 32


def inverse_kernel(first_ref, second_ref, third_ref, fourth_ref, count_ref, out_ref, work):
    order = out_ref.shape[0]
    rows = lax.broadcasted_iota(jnp.int32, (order, order), 0)
    columns = lax.broadcasted_iota(jnp.int32, (order, order), 1)
    row, column = columns[:1], rows[:, :1]
    total = (first_ref[...] + second_ref[...]) + (third_ref[...] + fourth_ref[...])
    work[...] = total / count_ref[0] + jnp.where(rows == columns, DAMPING, 0.0)

    def panel(_, carry):
        block = work[...]
        for k in range(0, PANEL, 2):
            n = k + 1
            a, b = block[k : k + 1, k : k + 1], block[k : k + 1, n : n + 1]
            c = block[n : n + 1, n : n + 1]
            scale = 1.0 / (a * c - b * b)
            row_k = jnp.where(row == k, -1.0, jnp.where(row == n, 0.0, block[k : k + 1, :]))
            row_n = jnp.where(row == n, -1.0, jnp.where(row == k, 0.0, block[n : n + 1, :]))
            column_k = jnp.where(column == k, -1.0, jnp.where(column == n, 0.0, block[:, k : k + 1]))
            column_n = jnp.where(column == n, -1.0, jnp.where(column == k, 0.0, block[:, n : n + 1]))
            solved_k = (c * row_k - b * row_n) * scale
            solved_n = (a * row_n - b * row_k) * scale
            outside = (rows // 2 != k // 2) & (columns // 2 != k // 2)
            block = jnp.where(outside, block, 0.0) - column_k * solved_k - column_n * solved_n
        rest = order - PANEL
        work[:rest, :rest] = block[PANEL:, PANEL:]
        work[:rest, rest:] = block[PANEL:, :PANEL]
        work[rest:, :rest] = block[:PANEL, PANEL:]
        work[rest:, rest:] = block[:PANEL, :PANEL]
        return carry

    lax.fori_loop(0, order // PANEL, panel, 0)
    out_ref[...] = (-work[...]).astype(bf16)


def invert_block(parts, counted):
    order = parts[0].shape[0]
    return pl.pallas_call(
        inverse_kernel,
        out_shape=jax.ShapeDtypeStruct((order, order), bf16),
        in_specs=[
            *[pl.BlockSpec(memory_space=pltpu.VMEM)] * 4,
            pl.BlockSpec(memory_space=pltpu.SMEM),
        ],
        out_specs=pl.BlockSpec(memory_space=pltpu.VMEM),
        scratch_shapes=[pltpu.VMEM((order, order), f32)],
        compiler_params=pltpu.CompilerParams(vmem_limit_bytes=GRANT),
    )(*parts, counted)


def swap_cores(array):
    count = lax.axis_size("section")
    return lax.ppermute(array, "section", [(i, i ^ 1) for i in range(count)])


def hop(array, source, by):
    pairs = [(2 * source + core, 2 * (source + by) + core) for core in range(2)]
    return lax.ppermute(array, "section", pairs)


GROUP = 8


def groups_near(count):
    return [list(range(base, base + GROUP)) for base in range(0, count, GROUP)]


def swap_groups(array, apart):
    count = lax.axis_size("dp")
    pairs = [(i, (i // GROUP ^ apart) * GROUP + i % GROUP) for i in range(count)]
    return lax.ppermute(array, "dp", pairs)


def halves(core, own, other):
    first = jnp.where(core == 0, own, other)
    second = jnp.where(core == 0, other, own)
    return jnp.concatenate([first, second], axis=1)


def spread(values):
    lines = groups_near(lax.axis_size("dp"))
    return lax.all_to_all(
        values, "dp", split_axis=1, concat_axis=0, axis_index_groups=lines, tiled=True
    )


def gather_back(values):
    lines = groups_near(lax.axis_size("dp"))
    return lax.all_to_all(
        values, "dp", split_axis=0, concat_axis=1, axis_index_groups=lines, tiled=True
    )


def gram_halves(taken, live, odd):
    masked = jnp.where(live, taken, jnp.zeros((), bf16))
    grams = []
    for b in range(2):
        part = masked[:, b * BLOCK : (b + 1) * BLOCK]
        grams.append(
            lax.dot_general(part, part, (((0,), (0,)), ((), ())), preferred_element_type=f32)
        )
    mine = jnp.where(odd, grams[1], grams[0])
    theirs = jnp.where(odd, grams[0], grams[1])
    return mine, theirs


def share_parts(mine, theirs):
    return (mine, swap_groups(theirs, 1), swap_groups(mine, 2), swap_groups(theirs, 3))


def invert_all(parts, counted, odd):
    inverse = invert_block(parts, counted)
    other = swap_groups(inverse, 1)
    return jnp.where(odd, other, inverse), jnp.where(odd, inverse, other)


def apply_blocks(taken, inverses):
    results = [
        jnp.dot(
            taken[:, b * BLOCK : (b + 1) * BLOCK], inverse, preferred_element_type=f32
        ).astype(bf16)
        for b, inverse in enumerate(inverses)
    ]
    return jnp.concatenate(results, axis=1)


def all_stages(inputs, cotangent, weights, lengths):
    section = lax.axis_index("section")
    chip, core = section // 2, section % 2
    chips = lax.axis_size("section") // 2
    tokens, width = inputs.shape
    half = width // 2
    batch_rows = tokens // lengths.shape[0]
    scalar_core = core.reshape(1).astype(jnp.int32)

    local = weights[0]
    mine = jnp.where(core == 0, local[:, :half], local[:, half:])
    theirs = jnp.where(core == 0, local[:, half:], local[:, :half])
    swapped = swap_cores(theirs)
    paired = jnp.concatenate([mine, swapped], axis=1)
    weight = lax.all_gather(paired, "dp", axis=0, tiled=True)

    all_lengths = lax.all_gather(lengths, "dp", axis=0)
    alive = jnp.clip(all_lengths, 0, batch_rows)
    counted = jnp.sum(alive).astype(f32).reshape(1)
    near = lax.axis_index("dp") // GROUP
    odd = near % 2 == 1
    line = lax.dynamic_index_in_dim(all_lengths.reshape(4, GROUP, -1), near, 0, keepdims=False)
    live = (jnp.arange(batch_rows)[None, :] < line.reshape(-1, 1)).reshape(-1, 1)

    def own_half(array):
        return jnp.where(core == 0, array[:, :half], array[:, half:])

    def other_half(array):
        return jnp.where(core == 0, array[:, half:], array[:, :half])

    first_own = own_half(inputs)
    first_own, counted, live = lax.optimization_barrier((first_own, counted, live))
    empty = jnp.zeros((tokens, half), bf16)
    kept = (empty, empty, empty, empty)
    arriving = first_own
    for stage in range(chips):
        last = stage == chips - 1

        def turn(operands, stage=stage, last=last):
            own, weight = operands
            other = other_half(inputs) if stage == 0 else swap_cores(own)
            second = forward_layer(scalar_core, own, other, weight, 0)
            second_other = swap_cores(second)
            if last:
                leaving = empty
            else:
                leaving = forward_layer(scalar_core, second, second_other, weight, 1)
            return (own, other, second, second_other), leaving

        def rest(operands, kept=kept):
            return kept, empty

        kept, leaving = lax.cond(chip == stage, turn, rest, (arriving, weight))
        if not last:
            arriving = hop(leaving, stage, 1)

    own_a, other_a, own_b, other_b = kept
    grads = (empty, empty)
    arriving = own_half(cotangent)
    pre_inputs = None
    taken = None
    for stage in range(chips - 1, -1, -1):

        def turn(operands, stage=stage):
            grad, own_a, other_a, own_b, other_b, weight = operands
            pieces = backward_layer(scalar_core, (grad,), own_b, other_b, weight, 1)
            if stage == 0:
                return (finish_layer(*pieces), grad), empty
            pieces = backward_layer(scalar_core, pieces, own_a, other_a, weight, 0)
            return (pieces[0], grad), finish_layer(*pieces)

        def rest(operands, grads=grads):
            return grads, empty

        grads, leaving = lax.cond(
            chip == stage, turn, rest, (arriving, own_a, other_a, own_b, other_b, weight)
        )
        if stage > 0:
            arriving = hop(leaving, stage, -1)
        if stage == chips - 1:
            own = jnp.where(core == 0, own_a, own_b)
            other = jnp.where(core == 0, other_a, other_b)
            own, other, leaving = lax.optimization_barrier((own, other, leaving))
            full = halves(core, own, other).astype(f32)
            mean = jnp.mean(full * full, axis=-1, keepdims=True)
            full = (full * lax.rsqrt(mean + EPSILON)).astype(bf16)
            taken = spread(full)
            parts = share_parts(*gram_halves(taken, live, odd))
            arriving, parts = lax.optimization_barrier((arriving, parts))
        elif stage == chips - 2:
            grads, parts = lax.optimization_barrier((grads, parts))
            inverses = invert_all(parts, counted, odd)
            pre_inputs = gather_back(apply_blocks(taken, inverses))
            arriving, pre_inputs = lax.optimization_barrier((arriving, pre_inputs))

    grad_a, grad_b = grads
    own = jnp.where(core == 0, grad_a, grad_b)
    other = swap_cores(jnp.where(core == 0, grad_b, grad_a))
    taken = spread(halves(core, own, other))
    inverses = invert_all(share_parts(*gram_halves(taken, live, odd)), counted, odd)
    pre_grads = gather_back(apply_blocks(taken, inverses))
    return (pre_inputs[None], pre_grads[None])


def solution(mesh):
    in_specs = (P("dp", None), P("dp", None), P("section", "dp", None), P("dp"))
    out_specs = (P("section", "dp", None), P("section", "dp", None))
    return jax.shard_map(
        all_stages, mesh=mesh, in_specs=in_specs, out_specs=out_specs, check_vma=False
    )
```

```python
import functools

import jax
import jax.numpy as jnp
from jax import lax
from jax.experimental import pallas as pl
from jax.experimental.pallas import tpu as pltpu
from jax.sharding import PartitionSpec as P


BLOCK = 160
EPSILON = 1e-05
DAMPING = 0.1
LANES = 128
GRANT = 44 * 1024 * 1024
TILE = 640
ROWS = 1280

f32 = jnp.float32
bf16 = jnp.bfloat16


def row_factor(own, other, width):
    total = jnp.sum(own * own, axis=-1, keepdims=True)
    total = total + jnp.sum(other * other, axis=-1, keepdims=True)
    return lax.rsqrt(total / width + EPSILON)


def forward_kernel(core_ref, own_ref, other_ref, wown_ref, wother_ref, out_ref, aown, aother):
    step = pl.program_id(0)
    half = own_ref.shape[1]

    @pl.when(step == 0)
    def _():
        own = own_ref[...].astype(f32)
        other = other_ref[...].astype(f32)
        factor = row_factor(own, other, 2 * half)
        aown[...] = (own * factor).astype(bf16)
        aother[...] = (other * factor).astype(bf16)

    result = jnp.dot(aown[...], wown_ref[...], preferred_element_type=f32)
    result = result + jnp.dot(aother[...], wother_ref[...], preferred_element_type=f32)
    columns = pl.ds(pl.multiple_of(step * TILE, TILE), TILE)
    out_ref[...] = (own_ref[:, columns].astype(f32) + result).astype(bf16)


def forward_layer(core, own, other, weight, which):
    rows, half = own.shape
    steps = half // TILE
    whole = pl.BlockSpec((rows, half), lambda i, c: (0, 0))

    def at(c):
        return 1 - c[0] if which else c[0]

    return pl.pallas_call(
        forward_kernel,
        out_shape=jax.ShapeDtypeStruct((rows, half), bf16),
        grid_spec=pltpu.PrefetchScalarGridSpec(
            num_scalar_prefetch=1,
            grid=(steps,),
            in_specs=[
                whole,
                whole,
                pl.BlockSpec((half, TILE), lambda i, c: (c[0], at(c) * steps + i)),
                pl.BlockSpec((half, TILE), lambda i, c: (1 - c[0], at(c) * steps + i)),
            ],
            out_specs=pl.BlockSpec((rows, TILE), lambda i, c: (0, i)),
            scratch_shapes=[pltpu.VMEM((rows, half), bf16), pltpu.VMEM((rows, half), bf16)],
        ),
        compiler_params=pltpu.CompilerParams(vmem_limit_bytes=GRANT),
        cost_estimate=pl.CostEstimate(
            flops=4 * rows * half * half, bytes_accessed=4 * half * half, transcendentals=0
        ),
    )(core, own, other, weight, weight)


def finish(grad, keep, arrived, own):
    half = own.shape[1]
    mine, theirs = keep[:, half + LANES :], arrived[:, half:].astype(f32)
    mean = jnp.sum(mine + theirs, axis=-1, keepdims=True) / (2 * half)
    factor = keep[:, half : half + 1]
    back = keep[:, :half] + arrived[:, :half].astype(f32)
    through = factor * (back - own.astype(f32) * factor * mean)
    return (grad.astype(f32) + through).astype(bf16)


def finish_kernel(grad_ref, keep_ref, arrived_ref, own_ref, out_ref):
    out_ref[...] = finish(grad_ref[...], keep_ref[...], arrived_ref[...], own_ref[...])


def finish_layer(grad, keep, arrived, own):
    rows, half = own.shape
    whole = pl.BlockSpec(memory_space=pltpu.VMEM)
    return pl.pallas_call(
        finish_kernel,
        out_shape=jax.ShapeDtypeStruct((rows, half), bf16),
        in_specs=[whole] * 4,
        out_specs=whole,
        compiler_params=pltpu.CompilerParams(vmem_limit_bytes=GRANT),
        cost_estimate=pl.CostEstimate(
            flops=8 * rows * half, bytes_accessed=16 * rows * half, transcendentals=0
        ),
    )(grad, keep, arrived, own)


def backward_kernel(fused, core_ref, *refs):
    if fused:
        before, refs = refs[:4], refs[4:]
        own_ref, other_ref, weight_ref, send_ref, keep_ref, grad_ref = refs
    else:
        grad_ref, own_ref, other_ref, weight_ref, send_ref, keep_ref = refs
    step = pl.program_id(0)
    rows, half = own_ref.shape
    steps = half // ROWS
    factor_at, product_at = slice(half, half + LANES), slice(half + LANES, half + 2 * LANES)

    @pl.when(step == 0)
    def _():
        if fused:
            grad_ref[...] = finish(*[ref[...] for ref in before])
        own = own_ref[...].astype(f32)
        other = other_ref[...].astype(f32)
        keep_ref[:, factor_at] = jnp.broadcast_to(row_factor(own, other, 2 * half), (rows, LANES))
        keep_ref[:, product_at] = jnp.zeros((rows, LANES), f32)

    part = lax.dot_general(
        grad_ref[...], weight_ref[...], (((1,), (1,)), ((), ())), preferred_element_type=f32
    )

    def along(hidden_ref, columns):
        product = part * hidden_ref[:, columns].astype(f32)
        folded = product[:, :LANES]
        for k in range(1, ROWS // LANES):
            folded = folded + product[:, k * LANES : (k + 1) * LANES]
        keep_ref[:, product_at] += folded * keep_ref[:, factor_at]

    @pl.when(step < steps)
    def _():
        columns = pl.ds(pl.multiple_of(step * ROWS, LANES), ROWS)
        send_ref[:, columns] = part.astype(bf16)
        along(other_ref, columns)

    @pl.when(step >= steps)
    def _():
        columns = pl.ds(pl.multiple_of((step - steps) * ROWS, LANES), ROWS)
        keep_ref[:, columns] = part
        along(own_ref, columns)

    @pl.when(step == 2 * steps - 1)
    def _():
        send_ref[:, half:] = keep_ref[:, product_at].astype(bf16)


def backward_layer(core, before, own, other, weight, which):
    rows, half = own.shape
    steps = half // ROWS
    fused = len(before) > 1

    def whole(extra=0):
        return pl.BlockSpec((rows, half + extra), lambda i, c: (0, 0))

    def place(i, c):
        return (jnp.where(i < steps, (1 - c[0]) * steps + i, c[0] * steps + i - steps), 1 - c[0] if which else c[0])

    out_shape = [
        jax.ShapeDtypeStruct((rows, half + LANES), bf16),
        jax.ShapeDtypeStruct((rows, half + 2 * LANES), f32),
    ]
    first = [whole(), whole(2 * LANES), whole(LANES), whole()] if fused else [whole()]
    results = pl.pallas_call(
        functools.partial(backward_kernel, fused),
        out_shape=out_shape + [jax.ShapeDtypeStruct((rows, half), bf16)] * fused,
        grid_spec=pltpu.PrefetchScalarGridSpec(
            num_scalar_prefetch=1,
            grid=(2 * steps,),
            in_specs=first + [whole(), whole(), pl.BlockSpec((ROWS, half), place)],
            out_specs=[whole(LANES), whole(2 * LANES)] + [whole()] * fused,
        ),
        compiler_params=pltpu.CompilerParams(vmem_limit_bytes=GRANT),
        cost_estimate=pl.CostEstimate(
            flops=4 * rows * half * half, bytes_accessed=4 * half * half, transcendentals=0
        ),
    )(core, *before, own, other, weight)
    send, keep = results[:2]
    grad = results[2] if fused else before[0]
    return (grad, keep, swap_cores(send), own)


PANEL = 32


def inverse_kernel(first_ref, second_ref, third_ref, fourth_ref, count_ref, out_ref, work):
    order = out_ref.shape[0]
    rows = lax.broadcasted_iota(jnp.int32, (order, order), 0)
    columns = lax.broadcasted_iota(jnp.int32, (order, order), 1)
    row, column = columns[:1], rows[:, :1]
    total = (first_ref[...] + second_ref[...]) + (third_ref[...] + fourth_ref[...])
    work[...] = total / count_ref[0] + jnp.where(rows == columns, DAMPING, 0.0)

    def panel(_, carry):
        block = work[...]
        for k in range(0, PANEL, 2):
            n = k + 1
            a, b = block[k : k + 1, k : k + 1], block[k : k + 1, n : n + 1]
            c = block[n : n + 1, n : n + 1]
            scale = 1.0 / (a * c - b * b)
            row_k = jnp.where(row == k, -1.0, jnp.where(row == n, 0.0, block[k : k + 1, :]))
            row_n = jnp.where(row == n, -1.0, jnp.where(row == k, 0.0, block[n : n + 1, :]))
            column_k = jnp.where(column == k, -1.0, jnp.where(column == n, 0.0, block[:, k : k + 1]))
            column_n = jnp.where(column == n, -1.0, jnp.where(column == k, 0.0, block[:, n : n + 1]))
            solved_k = (c * row_k - b * row_n) * scale
            solved_n = (a * row_n - b * row_k) * scale
            outside = (rows // 2 != k // 2) & (columns // 2 != k // 2)
            block = jnp.where(outside, block, 0.0) - column_k * solved_k - column_n * solved_n
        rest = order - PANEL
        work[:rest, :rest] = block[PANEL:, PANEL:]
        work[:rest, rest:] = block[PANEL:, :PANEL]
        work[rest:, :rest] = block[:PANEL, PANEL:]
        work[rest:, rest:] = block[:PANEL, :PANEL]
        return carry

    lax.fori_loop(0, order // PANEL, panel, 0)
    out_ref[...] = (-work[...]).astype(bf16)


def invert_block(parts, counted):
    order = parts[0].shape[0]
    return pl.pallas_call(
        inverse_kernel,
        out_shape=jax.ShapeDtypeStruct((order, order), bf16),
        in_specs=[
            *[pl.BlockSpec(memory_space=pltpu.VMEM)] * 4,
            pl.BlockSpec(memory_space=pltpu.SMEM),
        ],
        out_specs=pl.BlockSpec(memory_space=pltpu.VMEM),
        scratch_shapes=[pltpu.VMEM((order, order), f32)],
        compiler_params=pltpu.CompilerParams(vmem_limit_bytes=GRANT),
    )(*parts, counted)


def swap_cores(array):
    count = lax.axis_size("section")
    return lax.ppermute(array, "section", [(i, i ^ 1) for i in range(count)])


def hop(array, source, by):
    pairs = [(2 * source + core, 2 * (source + by) + core) for core in range(2)]
    return lax.ppermute(array, "section", pairs)


GROUP = 8


def groups_near(count):
    return [list(range(base, base + GROUP)) for base in range(0, count, GROUP)]


def swap_groups(array, apart):
    count = lax.axis_size("dp")
    pairs = [(i, (i // GROUP ^ apart) * GROUP + i % GROUP) for i in range(count)]
    return lax.ppermute(array, "dp", pairs)


def halves(core, own, other):
    first = jnp.where(core == 0, own, other)
    second = jnp.where(core == 0, other, own)
    return jnp.concatenate([first, second], axis=1)


def spread(values):
    lines = groups_near(lax.axis_size("dp"))
    return lax.all_to_all(
        values, "dp", split_axis=1, concat_axis=0, axis_index_groups=lines, tiled=True
    )


def gather_back(values):
    lines = groups_near(lax.axis_size("dp"))
    return lax.all_to_all(
        values, "dp", split_axis=0, concat_axis=1, axis_index_groups=lines, tiled=True
    )


def gram_halves(taken, live, odd):
    masked = jnp.where(live, taken, jnp.zeros((), bf16))
    grams = []
    for b in range(2):
        part = masked[:, b * BLOCK : (b + 1) * BLOCK]
        grams.append(
            lax.dot_general(part, part, (((0,), (0,)), ((), ())), preferred_element_type=f32)
        )
    mine = jnp.where(odd, grams[1], grams[0])
    theirs = jnp.where(odd, grams[0], grams[1])
    return mine, theirs


def share_parts(mine, theirs):
    far = swap_groups(mine, 2)
    near = (swap_groups(theirs, 1), swap_groups(theirs, 3))
    return (mine, far, *near)


def invert_all(parts, counted, odd):
    inverse = invert_block(parts, counted)
    other = swap_groups(inverse, 1)
    return jnp.where(odd, other, inverse), jnp.where(odd, inverse, other)


def apply_blocks(taken, inverses):
    results = [
        jnp.dot(
            taken[:, b * BLOCK : (b + 1) * BLOCK], inverse, preferred_element_type=f32
        ).astype(bf16)
        for b, inverse in enumerate(inverses)
    ]
    return jnp.concatenate(results, axis=1)


def all_stages(inputs, cotangent, weights, lengths):
    section = lax.axis_index("section")
    chip, core = section // 2, section % 2
    chips = lax.axis_size("section") // 2
    tokens, width = inputs.shape
    half = width // 2
    batch_rows = tokens // lengths.shape[0]
    scalar_core = core.reshape(1).astype(jnp.int32)

    local = weights[0]
    mine = jnp.where(core == 0, local[:, :half], local[:, half:])
    theirs = jnp.where(core == 0, local[:, half:], local[:, :half])
    swapped = swap_cores(theirs)
    paired = jnp.concatenate([mine, swapped], axis=1)
    weight = lax.all_gather(paired, "dp", axis=0, tiled=True)

    all_lengths = lax.all_gather(lengths, "dp", axis=0)
    alive = jnp.clip(all_lengths, 0, batch_rows)
    counted = jnp.sum(alive).astype(f32).reshape(1)
    near = lax.axis_index("dp") // GROUP
    odd = near % 2 == 1
    line = lax.dynamic_index_in_dim(all_lengths.reshape(4, GROUP, -1), near, 0, keepdims=False)
    live = (jnp.arange(batch_rows)[None, :] < line.reshape(-1, 1)).reshape(-1, 1)

    def own_half(array):
        return jnp.where(core == 0, array[:, :half], array[:, half:])

    def other_half(array):
        return jnp.where(core == 0, array[:, half:], array[:, :half])

    first_own = own_half(inputs)
    first_own, counted, live = lax.optimization_barrier((first_own, counted, live))
    empty = jnp.zeros((tokens, half), bf16)
    kept = (empty, empty, empty, empty)
    arriving = first_own
    for stage in range(chips):
        last = stage == chips - 1

        def turn(operands, stage=stage, last=last):
            own, weight = operands
            other = other_half(inputs) if stage == 0 else swap_cores(own)
            second = forward_layer(scalar_core, own, other, weight, 0)
            second_other = swap_cores(second)
            if last:
                leaving = empty
            else:
                leaving = forward_layer(scalar_core, second, second_other, weight, 1)
            return (own, other, second, second_other), leaving

        def rest(operands, kept=kept):
            return kept, empty

        kept, leaving = lax.cond(chip == stage, turn, rest, (arriving, weight))
        if not last:
            arriving = hop(leaving, stage, 1)

    own_a, other_a, own_b, other_b = kept
    grads = (empty, empty)
    arriving = own_half(cotangent)
    pre_inputs = None
    taken = None
    for stage in range(chips - 1, -1, -1):

        def turn(operands, stage=stage):
            grad, own_a, other_a, own_b, other_b, weight = operands
            pieces = backward_layer(scalar_core, (grad,), own_b, other_b, weight, 1)
            if stage == 0:
                return (finish_layer(*pieces), grad), empty
            pieces = backward_layer(scalar_core, pieces, own_a, other_a, weight, 0)
            return (pieces[0], grad), finish_layer(*pieces)

        def rest(operands, grads=grads):
            return grads, empty

        grads, leaving = lax.cond(
            chip == stage, turn, rest, (arriving, own_a, other_a, own_b, other_b, weight)
        )
        if stage > 0:
            arriving = hop(leaving, stage, -1)
        if stage == chips - 1:
            own = jnp.where(core == 0, own_a, own_b)
            other = jnp.where(core == 0, other_a, other_b)
            own, other, leaving = lax.optimization_barrier((own, other, leaving))
            full = halves(core, own, other).astype(f32)
            mean = jnp.mean(full * full, axis=-1, keepdims=True)
            full = (full * lax.rsqrt(mean + EPSILON)).astype(bf16)
            taken = spread(full)
            parts = share_parts(*gram_halves(taken, live, odd))
            arriving, parts = lax.optimization_barrier((arriving, parts))
        elif stage == chips - 2:
            grads, parts = lax.optimization_barrier((grads, parts))
            inverses = invert_all(parts, counted, odd)
            pre_inputs = gather_back(apply_blocks(taken, inverses))
            arriving, pre_inputs = lax.optimization_barrier((arriving, pre_inputs))

    grad_a, grad_b = grads
    own = jnp.where(core == 0, grad_a, grad_b)
    other = swap_cores(jnp.where(core == 0, grad_b, grad_a))
    taken = spread(halves(core, own, other))
    inverses = invert_all(share_parts(*gram_halves(taken, live, odd)), counted, odd)
    pre_grads = gather_back(apply_blocks(taken, inverses))
    return (pre_inputs[None], pre_grads[None])


def solution(mesh):
    in_specs = (P("dp", None), P("dp", None), P("section", "dp", None), P("dp"))
    out_specs = (P("section", "dp", None), P("section", "dp", None))
    return jax.shard_map(
        all_stages, mesh=mesh, in_specs=in_specs, out_specs=out_specs, check_vma=False
    )
```
